1024 devices in a mesh: grp: 32 (over z), srv: 32 (over x, y, core).
Axes of the slice: x: 4, y: 4, z: 32, core: 2. Of those that a mesh axis runs over, the one named last changes fastest.
Arguments:
- queries: bfloat16 [8192, 8192], P('srv', 'grp'), may hold values from -8 to 8
- key_rows: bfloat16 [8192, 1024], P('srv'), may hold values from -8 to 8
- value_rows: bfloat16 [8192, 1024], P('srv'), may hold values from -6 to 6
- grad_output: bfloat16 [8192, 8192], P('srv', 'grp'), may hold values from -6 to 6
- doc_ids: int32 [8192], replicated, may hold values from 0 to 31, never falling along the last dimension, each value on 1 to 4352 neighbouring positions
Outputs:
- grad_query: bfloat16 [8192, 8192], P('srv', 'grp')
- grad_key: bfloat16 [8192, 1024], P('srv', 'grp')
- grad_value: bfloat16 [8192, 1024], P('srv', 'grp')
The draws below stay inside these ranges and needn't reach their ends.
Inputs may be any that keep to these rules, and one draw needn't show every extreme that they name: `doc_ids`: document numbers never fall along the pack; each document has 1 to 4352 tokens, and one has exactly 4352.
All inputs are finite; a program needn't handle non-finite values.
Results may differ from the reference program's by a relative error of at most 0.0069.
Values may be sent and summed in bfloat16 or wider, within the bound.
A program may use at most 32 MiB of HBM per device.

```python
import math
import jax
import jax.numpy as jnp
import numpy as np
from jax import lax

HD = 128
H = 64
KVH = 8
TOKENS = 8192
DOC_MOST = 4352
DOC_COUNT = 32


def draw_queries(key, part):
    base = jax.random.normal(jax.random.fold_in(key, 2), (TOKENS, H * HD), jnp.float32)
    return base.astype(jnp.bfloat16)


def draw_key_rows(key, part):
    base = jax.random.normal(jax.random.fold_in(key, 1), (TOKENS, KVH * HD), jnp.float32)
    return base.astype(jnp.bfloat16)


def shard_levels(key, shape, shards, least, high):
    def one(dim, shards_of):
        heights = jax.random.uniform(jax.random.fold_in(jax.random.fold_in(key, 6), dim), (shards_of,), jnp.float32, least / len(shards), high / len(shards))
        return jnp.repeat(jnp.exp(heights), shape[dim] // shards_of).reshape((-1,) + (1,) * (len(shape) - dim - 1))

    level = one(*shards[0])
    for cut in shards[1:]:
        level = level * one(*cut)
    return level


def split_up(count, total, most, skew):
    portions = [(1 << 20) // math.isqrt(grade ** skew) + 1 for grade in range(2, count + 1)]
    spare, holding = total - most - (count - 1), [1] * (count - 1)
    while spare > 0:
        movable = [i for i in range(count - 1) if holding[i] < most]
        pool, left = sum([portions[i] for i in movable]), spare
        for i in movable:
            extra = min(most - holding[i], max(1, left * portions[i] // pool), spare)
            holding[i] = holding[i] + extra
            spare = spare - extra
    return np.array([most] + holding)


def ragged_sizes(stream_key, amount, total, limit, lean):
    if amount == 2:
        one = jax.random.randint(stream_key, (), max(1, total - limit), min(limit, total - 1) + 1)
        return jnp.stack([one, total - one])
    lengths = jnp.asarray(split_up(amount, total, limit, lean), jnp.int32)
    pairs = (amount - 1) // 2
    donor, receiver = lengths[1:1 + 2 * pairs:2], lengths[2:2 + 2 * pairs:2]
    margin = jnp.minimum(donor - 1, limit - receiver)
    shifted = jax.random.randint(jax.random.fold_in(stream_key, 1), (pairs,), 0, 1 << 20) % (margin + 1)
    lengths = lengths.at[1:1 + 2 * pairs:2].set(donor - shifted).at[2:2 + 2 * pairs:2].set(receiver + shifted)
    return lengths[jax.random.permutation(jax.random.fold_in(stream_key, 2), amount)]


def noise(own_key, extent, spread, reach, cuts=(), kind=jnp.bfloat16):
    values = spread * jax.random.normal(own_key, extent, jnp.float32)
    if cuts:
        values = values * shard_levels(own_key, extent, cuts, -0.22, 0.18)
    return jnp.clip(values, -reach, reach).astype(kind)


def setup_inputs(seed: int = 0) -> dict:
    splits = jax.random.split(jax.random.key(seed), 6)
    return {
        "queries": draw_queries(jax.random.fold_in(splits[5], 71), 0),
        "key_rows": draw_key_rows(jax.random.fold_in(splits[5], 71), 0),
        "value_rows": noise(splits[2], (TOKENS, KVH * HD), 1.0, 6.0, ((0, 32),)),
        "grad_output": noise(splits[3], (TOKENS, H * HD), 1.0, 6.0, ((0, 32), (1, 32))),
        "doc_ids": jnp.searchsorted(jnp.cumsum(ragged_sizes(splits[4], DOC_COUNT, TOKENS, DOC_MOST, 2)), jnp.arange(TOKENS), side="right").astype(jnp.int32),
    }


big_negative = -1.0e30


def reference(queries, key_rows, value_rows, grad_output, doc_ids):
    score_scale = HD ** -0.5
    ratio = H // KVH
    positions = jnp.arange(TOKENS, dtype=jnp.int32)
    allowed = (doc_ids[:, None] == doc_ids[None, :]) & (positions[None, :] <= positions[:, None])

    def one_head(head_index):
        kv_index = head_index // ratio
        query_head = lax.dynamic_slice_in_dim(queries, head_index * HD, HD, 1)
        grad_head = lax.dynamic_slice_in_dim(grad_output, head_index * HD, HD, 1)
        key_head = lax.dynamic_slice_in_dim(key_rows, kv_index * HD, HD, 1)
        value_head = lax.dynamic_slice_in_dim(value_rows, kv_index * HD, HD, 1)
        scores = jnp.dot(query_head, key_head.T, preferred_element_type=jnp.float32) * score_scale
        masked = jnp.where(allowed, scores, big_negative)
        row_max = jnp.max(masked, axis=1, keepdims=True)
        row_sum = jnp.sum(jnp.where(allowed, jnp.exp(masked - row_max), 0.0), axis=1, keepdims=True)
        log_norm = row_max + jnp.log(row_sum)
        weights = jnp.where(allowed, jnp.exp(scores - log_norm), 0.0)
        grad_probs = jnp.dot(grad_head, value_head.T, preferred_element_type=jnp.float32)
        row_delta = jnp.sum(weights * grad_probs, axis=1, keepdims=True)
        grad_scores = (weights * (grad_probs - row_delta)).astype(jnp.bfloat16)
        weights_low = weights.astype(jnp.bfloat16)
        grad_query = (jnp.dot(grad_scores, key_head, preferred_element_type=jnp.float32) * score_scale).astype(jnp.bfloat16)
        grad_key = jnp.dot(grad_scores.T, query_head, preferred_element_type=jnp.float32) * score_scale
        grad_value = jnp.dot(weights_low.T, grad_head, preferred_element_type=jnp.float32)
        return grad_query, grad_key, grad_value

    grad_query, grad_key, grad_value = lax.map(one_head, jnp.arange(H, dtype=jnp.int32))
    grad_query = grad_query.transpose(1, 0, 2).reshape(TOKENS, H * HD)
    grad_key = grad_key.reshape(KVH, ratio, TOKENS, HD).sum(axis=1)
    grad_value = grad_value.reshape(KVH, ratio, TOKENS, HD).sum(axis=1)
    grad_key = grad_key.transpose(1, 0, 2).reshape(TOKENS, KVH * HD).astype(jnp.bfloat16)
    grad_value = grad_value.transpose(1, 0, 2).reshape(TOKENS, KVH * HD).astype(jnp.bfloat16)
    return (grad_query, grad_key, grad_value)
```

```python
import functools
import math

import jax
import jax.numpy as jnp
from jax import lax
from jax.experimental import pallas as pl
from jax.experimental.pallas import tpu as pltpu
from jax.sharding import PartitionSpec as P

HD = 128
SIDE = 4
REACH = 9
HIDDEN = -1e30
MESH = pl.DeviceIdType.MESH
SCALE = HD ** -0.5
SCALE2 = SCALE * math.log2(math.e)


def kernel(
    share, q_ref, k_ref, v_ref, o_ref, doc_ref,
    dq_out, dk_out, dv_out,
    kv, qc, oc, qt, ot, low, high, prob, dprob, mrun, stat, stat_in,
    dqt, dq_in, part, got, accf, xout, xin, zown, zout, zin,
    loc_sem, qs_sem, qr_sem, ks_sem, kr_sem, ss_sem, sr_sem, ps_sem, pr_sem,
    xs_sem, xr_sem, zs_sem, zr_sem, ds_sem, dr_sem,
):
    R = q_ref.shape[0]
    grp = lax.axis_index("grp")
    srv = lax.axis_index("srv")
    core = lax.rem(srv, 2)
    chip = lax.div(srv, 2)
    y = lax.rem(chip, SIDE)
    x = lax.div(chip, SIDE)
    member = lax.rem(grp, share)
    kv_head = lax.div(grp, share)
    mate = srv + 1 - 2 * core

    def at(cx, cy):
        return (grp, (cx * SIDE + cy) * 2 + core)

    def remote(src, dst, ssem, rsem, device):
        return pltpu.make_async_remote_copy(
            src_ref=src, dst_ref=dst, send_sem=ssem, recv_sem=rsem,
            device_id=device, device_id_type=MESH,
        )

    col = pl.ds(pl.multiple_of(kv_head * HD, HD), HD)
    mine = pl.multiple_of(core * (2 * R), 2 * R)
    local = [
        pltpu.make_async_copy(k_ref.at[:, col], kv.at[0, :, pl.ds(0, HD)], loc_sem.at[0]),
        pltpu.make_async_copy(v_ref.at[:, col], kv.at[0, :, pl.ds(HD, HD)], loc_sem.at[1]),
    ]
    for h in range(2):
        rows = pl.ds(mine + h * R, R)
        cols = pl.ds(h * HD, HD)
        local.append(pltpu.make_async_copy(q_ref.at[:, cols], qc.at[rows], loc_sem.at[2 + 2 * h]))
        local.append(pltpu.make_async_copy(o_ref.at[:, cols], oc.at[rows], loc_sem.at[3 + 2 * h]))
    for copy in local:
        copy.start()

    barrier = pltpu.get_barrier_semaphore()

    def greet(device):
        pl.semaphore_signal(barrier, inc=1, device_id=device, device_id_type=MESH)

    far_out = (chip == 3) & (core == 1)
    far_in = (chip == 12) & (core == 1)
    greet((grp, mate))
    for e in range(1, SIDE):
        greet(at(x, lax.rem(y + e, SIDE)))
        greet(at(lax.rem(x + e, SIDE), y))
    for e in range(1, share):
        greet((grp - member + lax.rem(member + e, share), srv))

    @pl.when(far_out)
    def _():
        greet(at(3, 0))

    @pl.when(far_in)
    def _():
        greet(at(0, 3))

    wide = doc_ref.shape[1]
    number = lax.broadcasted_iota(jnp.int32, (32, wide), 0)
    count = jnp.zeros((32, wide), jnp.int32)
    for r in range(doc_ref.shape[0]):
        count = count + (doc_ref[pl.ds(r, 1), :] < number).astype(jnp.int32)
    first = jnp.sum(count, axis=1, keepdims=True)
    lane = lax.broadcasted_iota(jnp.int32, (1, wide), 1)
    per = R // wide
    for b in range(2):
        for t in range(per):
            row = (chip * 2 + b) * per + t
            own = doc_ref[pl.ds(row, 1), :]
            begin = jnp.sum(jnp.where(own == number, first, 0), axis=0, keepdims=True)
            for h in range(2):
                sl = pl.ds(b * 2 * R + h * R + t * wide, wide)
                low[:, sl] = begin
                high[:, sl] = lane + row * wide

    stat[0:1, :] = jnp.full((1, 4 * R), HIDDEN, jnp.float32)
    stat[1:3, :] = jnp.zeros((2, 4 * R), jnp.float32)
    dqt[...] = jnp.zeros_like(dqt)

    far = jnp.where(far_out | far_in, 1, 0)
    pl.semaphore_wait(barrier, 1 + 2 * (SIDE - 1) + share - 1 + far)

    for copy in local[:2]:
        copy.wait()

    def kv_send(slot, d, n, device):
        return remote(kv.at[slot], kv.at[d], ks_sem.at[n], kr_sem.at[d], device)

    own_sends = []
    for e in range(1, 3):
        own_sends.append((x + e < SIDE, kv_send(0, 4 * e, e - 1, at(lax.rem(x + e, SIDE), y))))
    own_sends.append((far_out, kv_send(0, 9, 2, at(3, 0))))
    for e in range(1, SIDE):
        own_sends.append((y + e < SIDE, kv_send(0, e, 2 + e, at(x, lax.rem(y + e, SIDE)))))
    near_sends = []
    for e in range(1, SIDE):
        near_sends.append(
            (x >= 1, kv_send(4, lax.rem(y + e, SIDE) - y + 4, 5 + e, at(x, lax.rem(y + e, SIDE))))
        )
    next_sends = []
    for e in range(1, SIDE):
        wraps = y + e >= SIDE
        cond = (x >= 2) & (wraps | (core == 1) if e == 1 else wraps)
        next_sends.append(
            (cond, kv_send(8, lax.rem(lax.rem(y + e, SIDE) - y + 8, 10), 8 + e, at(x, lax.rem(y + e, SIDE))))
        )

    def start_all(sends):
        for cond, copy in sends:
            pl.when(cond)(copy.start)

    start_all(own_sends)
    for copy in local[2:]:
        copy.wait()
    q_swap = remote(qc.at[pl.ds(mine, 2 * R)], qc.at[pl.ds(mine, 2 * R)], qs_sem.at[0], qr_sem.at[0], (grp, mate))
    o_swap = remote(oc.at[pl.ds(mine, 2 * R)], oc.at[pl.ds(mine, 2 * R)], qs_sem.at[1], qr_sem.at[1], (grp, mate))
    q_swap.start()
    o_swap.start()
    q_swap.wait()
    o_swap.wait()
    qt[...] = qc[...].T
    ot[...] = oc[...].T

    def kv_arrived(d):
        remote(kv.at[d], kv.at[d], ks_sem.at[0], kr_sem.at[d], (grp, mate)).wait_recv()

    row_in_block = lax.broadcasted_iota(jnp.int32, (R, R), 0)

    def stats_step(d, carry):
        @pl.when((d == 1) & (x >= 1))
        def _():
            kv_arrived(4)
            start_all(near_sends)

        @pl.when((d == 3) & (x >= 2))
        def _():
            kv_arrived(8)
            start_all(next_sends)

        @pl.when(chip >= d)
        def _():
            @pl.when(lax.rem(d, 4) != 0)
            def _():
                kv_arrived(d)

            key_pos = row_in_block + ((chip - d) * 2 + core) * R
            keys = kv[d, :, 0:HD]
            values = kv[d, :, HD:2 * HD]
            for g in range(4):
                sl = slice(g * R, (g + 1) * R)
                s = jnp.dot(keys, qt[:, sl], preferred_element_type=jnp.float32) * SCALE2
                ok = (key_pos >= low[:, sl]) & (key_pos <= high[:, sl])
                s = jnp.where(ok, s, HIDDEN)
                m_old = stat[0:1, sl]
                m_new = jnp.maximum(m_old, jnp.max(s, axis=0, keepdims=True))
                alpha = jnp.exp2(m_old - m_new)
                p = jnp.exp2(s - m_new)
                dp = jnp.dot(values, ot[:, sl], preferred_element_type=jnp.float32)
                stat[0:1, sl] = m_new
                stat[1:2, sl] = stat[1:2, sl] * alpha + jnp.sum(p, axis=0, keepdims=True)
                stat[2:3, sl] = stat[2:3, sl] * alpha + jnp.sum(p * dp, axis=0, keepdims=True)
                mrun[d, :, sl] = m_new
                prob[d, :, sl] = p
                dprob[d, :, sl] = dp

        return carry

    lax.fori_loop(0, 9 + core, stats_step, 0)

    stat_swap = remote(stat, stat_in, ss_sem, sr_sem, (grp, mate))
    stat_swap.start()
    stat_swap.wait()
    m_all = jnp.maximum(stat[0:1, :], stat_in[0:1, :])
    here = jnp.exp2(stat[0:1, :] - m_all)
    there = jnp.exp2(stat_in[0:1, :] - m_all)
    total = stat[1:2, :] * here + stat_in[1:2, :] * there
    weighted = stat[2:3, :] * here + stat_in[2:3, :] * there
    stat[4:5, :] = m_all + jnp.log2(total)
    stat[5:6, :] = weighted / total

    def part_copy(d):
        owner = chip - d
        oy = lax.rem(owner, SIDE)
        a = x - lax.div(owner, SIDE)
        tx = x - 3 * lax.div(a, 3)
        return remote(part.at[d], got.at[a, y], ps_sem.at[d], pr_sem.at[a, y], at(tx, oy))

    def grads_step(i, carry):
        d = 8 + core - i

        @pl.when(chip >= d)
        def _():
            plow, slow = [], []
            for g in range(4):
                sl = slice(g * R, (g + 1) * R)
                factor = jnp.exp2(mrun[d, :, sl] - stat[4:5, sl])
                p = prob[d, :, sl] * factor
                plow.append(p.astype(jnp.bfloat16))
                slow.append((p * (dprob[d, :, sl] - stat[5:6, sl])).astype(jnp.bfloat16))
            keys = kv[d, :, 0:HD]
            for b in range(2):
                dqt[b] += lax.dot_general(
                    keys, jnp.concatenate(slow[2 * b:2 * b + 2], axis=1),
                    (((0,), (0,)), ((), ())), preferred_element_type=jnp.float32,
                )
            dk = jnp.dot(jnp.concatenate(slow, axis=1), qc[...], preferred_element_type=jnp.float32)
            dv = jnp.dot(jnp.concatenate(plow, axis=1), oc[...], preferred_element_type=jnp.float32)

            @pl.when(lax.rem(d, 4) == 0)
            def _():
                accf[lax.div(d, 4), :, 0:HD] = dk
                accf[lax.div(d, 4), :, HD:2 * HD] = dv

            @pl.when(lax.rem(d, 4) != 0)
            def _():
                part[d, :, 0:HD] = dk.astype(jnp.bfloat16)
                part[d, :, HD:2 * HD] = dv.astype(jnp.bfloat16)
                part_copy(d).start()

        return carry

    lax.fori_loop(0, 9 + core, grads_step, 0)

    dq_swap = remote(dqt.at[1 - core], dq_in, ds_sem, dr_sem, (grp, mate))
    dq_swap.start()

    def part_arrived(a, sy):
        remote(got.at[a, sy], got.at[a, sy], ps_sem.at[0], pr_sem.at[a, sy], (grp, mate)).wait_recv()

    def gather_row(a, e, cond):
        sy = lax.rem(y + e, SIDE)

        @pl.when(cond)
        def _():
            part_arrived(a, sy)
            accf[a] += got[a, sy].astype(jnp.float32)

    x_sends = []
    for a in (2, 1):
        for e in range(1, SIDE):
            wraps = y + e >= SIDE
            if a == 1:
                cond = x >= 1
            else:
                cond = (x >= 2) & (wraps | (core == 1) if e == 1 else wraps)
            gather_row(a, e, cond)
        copy = remote(xout.at[a - 1], xin.at[a - 1], xs_sem.at[a - 1], xr_sem.at[a - 1], at(lax.rem(x - a + SIDE, SIDE), y))
        x_sends.append((x >= a, copy))

        @pl.when(x >= a)
        def _():
            xout[a - 1] = accf[a].astype(jnp.bfloat16)
            copy.start()

    for e in range(1, SIDE):
        gather_row(0, e, y + e < SIDE)

    dq_swap.wait()
    mixed = dqt[core] + dq_in[...]
    for h in range(2):
        dq_out[:, h * HD:(h + 1) * HD] = (mixed[:, h * R:(h + 1) * R].T * SCALE).astype(jnp.bfloat16)

    for a in (1, 2):
        @pl.when(x + a < SIDE)
        def _():
            remote(xin.at[a - 1], xin.at[a - 1], xs_sem.at[0], xr_sem.at[a - 1], (grp, mate)).wait_recv()
            accf[0] += xin[a - 1].astype(jnp.float32)

    @pl.when(far_out)
    def _():
        part_arrived(3, 0)
        accf[0] += got[3, 0].astype(jnp.float32)

    wide_out = HD // share
    turned = accf[0].T
    for m in range(share):
        for s in range(2):
            piece = turned[s * HD + m * wide_out:s * HD + (m + 1) * wide_out, :]
            zown[m, s * wide_out:(s + 1) * wide_out, :] = piece
            zout[m, s * wide_out:(s + 1) * wide_out, :] = piece.astype(jnp.bfloat16)
    z_sends = []
    for e in range(1, share):
        to = lax.rem(member + e, share)
        z_sends.append(
            remote(zout.at[to], zin.at[member], zs_sem.at[to], zr_sem.at[member], (grp - member + to, srv))
        )
    for copy in z_sends:
        copy.start()
    result = zown[member]
    for e in range(1, share):
        sender = lax.rem(member + e, share)
        remote(zin.at[sender], zin.at[sender], zs_sem.at[0], zr_sem.at[sender], (grp, mate)).wait_recv()
        result = result + zin[sender].astype(jnp.float32)
    dk_out[...] = (result[0:wide_out].T * SCALE).astype(jnp.bfloat16)
    dv_out[...] = result[wide_out:2 * wide_out].T.astype(jnp.bfloat16)

    for cond, copy in own_sends + near_sends + next_sends + x_sends:
        pl.when(cond)(copy.wait_send)

    def parts_sent(d, carry):
        @pl.when((chip >= d) & (lax.rem(d, 4) != 0))
        def _():
            part_copy(d).wait_send()

        return carry

    lax.fori_loop(1, 9 + core, parts_sent, 0)
    for copy in z_sends:
        copy.wait_send()


def on_device(queries, key_rows, value_rows, grad_output, doc_ids):
    R = queries.shape[0]
    share = lax.axis_size("grp") // (key_rows.shape[1] // HD)
    wide = min(128, R)
    docs = doc_ids.reshape(-1, wide)
    bf, f32, i32 = jnp.bfloat16, jnp.float32, jnp.int32
    dma = pltpu.SemaphoreType.DMA
    scratch = [
        pltpu.VMEM((10, R, 2 * HD), bf),
        pltpu.VMEM((4 * R, HD), bf),
        pltpu.VMEM((4 * R, HD), bf),
        pltpu.VMEM((HD, 4 * R), bf),
        pltpu.VMEM((HD, 4 * R), bf),
        pltpu.VMEM((1, 4 * R), i32),
        pltpu.VMEM((1, 4 * R), i32),
        pltpu.VMEM((10, R, 4 * R), f32),
        pltpu.VMEM((10, R, 4 * R), f32),
        pltpu.VMEM((10, 1, 4 * R), f32),
        pltpu.VMEM((8, 4 * R), f32),
        pltpu.VMEM((8, 4 * R), f32),
        pltpu.VMEM((2, HD, 2 * R), f32),
        pltpu.VMEM((HD, 2 * R), f32),
        pltpu.VMEM((10, R, 2 * HD), bf),
        pltpu.VMEM((4, SIDE, R, 2 * HD), bf),
        pltpu.VMEM((3, R, 2 * HD), f32),
        pltpu.VMEM((2, R, 2 * HD), bf),
        pltpu.VMEM((2, R, 2 * HD), bf),
        pltpu.VMEM((share, 2 * HD // share, R), f32),
        pltpu.VMEM((share, 2 * HD // share, R), bf),
        pltpu.VMEM((share, 2 * HD // share, R), bf),
        dma((6,)), dma((2,)), dma((2,)), dma((12,)), dma((10,)), dma(()), dma(()),
        dma((10,)), dma((4, SIDE)), dma((2,)), dma((2,)), dma((share,)), dma((share,)),
        dma(()), dma(()),
    ]
    vmem = pl.BlockSpec(memory_space=pltpu.VMEM)
    hbm = pl.BlockSpec(memory_space=pl.ANY)
    return pl.pallas_call(
        functools.partial(kernel, share),
        out_shape=(
            jax.ShapeDtypeStruct((R, 2 * HD), bf),
            jax.ShapeDtypeStruct((R, HD // share), bf),
            jax.ShapeDtypeStruct((R, HD // share), bf),
        ),
        in_specs=[hbm, hbm, hbm, hbm, vmem],
        out_specs=(vmem, vmem, vmem),
        scratch_shapes=scratch,
        compiler_params=pltpu.CompilerParams(
            collective_id=0, has_side_effects=True, vmem_limit_bytes=48 * 1024 * 1024
        ),
    )(queries, key_rows, value_rows, grad_output, docs)


def solution(mesh):
    in_specs = (P("srv", "grp"), P("srv", None), P("srv", None), P("srv", "grp"), P())
    out_specs = (P("srv", "grp"), P("srv", "grp"), P("srv", "grp"))
    return jax.shard_map(
        on_device, mesh=mesh, in_specs=in_specs, out_specs=out_specs, check_vma=False
    )
```

```python
import functools
import math

import jax
import jax.numpy as jnp
from jax import lax
from jax.experimental import pallas as pl
from jax.experimental.pallas import tpu as pltpu
from jax.sharding import PartitionSpec as P

HD = 128
SIDE = 4
REACH = 9
HIDDEN = -1e30
MESH = pl.DeviceIdType.MESH
SCALE = HD ** -0.5
SCALE2 = SCALE * math.log2(math.e)


def kernel(
    share, q_ref, k_ref, v_ref, o_ref, doc_ref,
    dq_out, dk_out, dv_out,
    kv, qc, oc, qt, ot, low, high, prob, dprob, mrun, stat, stat_in,
    dqt, dq_in, part, got, accf, zown, zout, zin,
    loc_sem, qs_sem, qr_sem, ks_sem, kr_sem, ss_sem, sr_sem, ps_sem, pr_sem,
    zs_sem, zr_sem, ds_sem, dr_sem,
):
    R = q_ref.shape[0]
    grp = lax.axis_index("grp")
    srv = lax.axis_index("srv")
    core = lax.rem(srv, 2)
    chip = lax.div(srv, 2)
    y = lax.rem(chip, SIDE)
    x = lax.div(chip, SIDE)
    member = lax.rem(grp, share)
    kv_head = lax.div(grp, share)
    mate = srv + 1 - 2 * core

    def at(cx, cy):
        return (grp, (cx * SIDE + cy) * 2 + core)

    def remote(src, dst, ssem, rsem, device):
        return pltpu.make_async_remote_copy(
            src_ref=src, dst_ref=dst, send_sem=ssem, recv_sem=rsem,
            device_id=device, device_id_type=MESH,
        )

    col = pl.ds(pl.multiple_of(kv_head * HD, HD), HD)
    mine = pl.multiple_of(core * (2 * R), 2 * R)
    local = [
        pltpu.make_async_copy(k_ref.at[:, col], kv.at[0, :, pl.ds(0, HD)], loc_sem.at[0]),
        pltpu.make_async_copy(v_ref.at[:, col], kv.at[0, :, pl.ds(HD, HD)], loc_sem.at[1]),
    ]
    for h in range(2):
        rows = pl.ds(mine + h * R, R)
        cols = pl.ds(h * HD, HD)
        local.append(pltpu.make_async_copy(q_ref.at[:, cols], qc.at[rows], loc_sem.at[2 + 2 * h]))
        local.append(pltpu.make_async_copy(o_ref.at[:, cols], oc.at[rows], loc_sem.at[3 + 2 * h]))
    for copy in local:
        copy.start()

    barrier = pltpu.get_barrier_semaphore()

    def greet(device):
        pl.semaphore_signal(barrier, inc=1, device_id=device, device_id_type=MESH)

    far_out = (chip == 3) & (core == 1)
    far_in = (chip == 12) & (core == 1)
    greet((grp, mate))
    for e in range(1, SIDE):
        greet(at(x, lax.rem(y + e, SIDE)))
        greet(at(lax.rem(x + e, SIDE), y))
    for e in range(1, share):
        greet((grp - member + lax.rem(member + e, share), srv))

    @pl.when(far_out)
    def _():
        greet(at(3, 0))

    @pl.when(far_in)
    def _():
        greet(at(0, 3))

    wide = doc_ref.shape[1]
    number = lax.broadcasted_iota(jnp.int32, (32, wide), 0)
    count = jnp.zeros((32, wide), jnp.int32)
    for r in range(doc_ref.shape[0]):
        count = count + (doc_ref[pl.ds(r, 1), :] < number).astype(jnp.int32)
    first = jnp.sum(count, axis=1, keepdims=True)
    lane = lax.broadcasted_iota(jnp.int32, (1, wide), 1)
    per = R // wide
    for b in range(2):
        for t in range(per):
            row = (chip * 2 + b) * per + t
            own = doc_ref[pl.ds(row, 1), :]
            begin = jnp.sum(jnp.where(own == number, first, 0), axis=0, keepdims=True)
            for h in range(2):
                sl = pl.ds(b * 2 * R + h * R + t * wide, wide)
                low[:, sl] = begin
                high[:, sl] = lane + row * wide

    stat[0:1, :] = jnp.full((1, 4 * R), HIDDEN, jnp.float32)
    stat[1:3, :] = jnp.zeros((2, 4 * R), jnp.float32)
    dqt[...] = jnp.zeros_like(dqt)

    far = jnp.where(far_out | far_in, 1, 0)
    pl.semaphore_wait(barrier, 1 + 2 * (SIDE - 1) + share - 1 + far)

    for copy in local[:2]:
        copy.wait()

    up, down = lax.rem(y + 1, SIDE), lax.rem(y + SIDE - 1, SIDE)
    x_up, x_down = lax.rem(x + 1, SIDE), lax.rem(x + SIDE - 1, SIDE)
    middle = (y == 1) | (y == 2)

    def kv_send(n, slot, d, device):
        return remote(kv.at[slot], kv.at[d], ks_sem.at[n], kr_sem.at[d], device)

    own_sends = [
        (x < SIDE - 1, kv_send(0, 0, 4, at(x_up, y))),
        (y < SIDE - 1, kv_send(1, 0, 1, at(x, up))),
        (y == 0, kv_send(2, 0, 3, at(x, down))),
        (far_out, kv_send(3, 0, 9, at(3, 0))),
    ]
    own_relay = [(middle, kv_send(4, 1, 2, at(x, up)))]
    near_sends = [
        ((x >= 1) & (x < SIDE - 1), kv_send(5, 4, 8, at(x_up, y))),
        (x >= 1, kv_send(6, 4, 4 + up - y, at(x, up))),
        (x >= 1, kv_send(7, 4, 4 + down - y, at(x, down))),
    ]
    near_slot = 4 + y - up
    near_relay = [(x >= 1, kv_send(8, near_slot, 4 + down - up, at(x, down)))]
    next_sends = [
        ((x >= 2) & (y >= 1), kv_send(9, 8, 7, at(x, down))),
        ((x >= 2) & (y == SIDE - 1), kv_send(10, 8, 5, at(x, up))),
        ((x >= 2) & (y < SIDE - 1) & (core == 1), kv_send(11, 8, 9, at(x, up))),
    ]
    next_relay = [((x >= 2) & middle, kv_send(12, 7, 6, at(x, down)))]

    def early(d):
        return (
            (d == 4) | (d == 8) | ((d == 1) & middle)
            | ((d == 3) & (y < SIDE - 1)) | ((d == 7) & (y >= 1))
        )

    def start_all(sends):
        for cond, copy in sends:
            pl.when(cond)(copy.start)

    start_all(own_sends)
    for copy in local[2:]:
        copy.wait()
    q_swap = remote(qc.at[pl.ds(mine, 2 * R)], qc.at[pl.ds(mine, 2 * R)], qs_sem.at[0], qr_sem.at[0], (grp, mate))
    o_swap = remote(oc.at[pl.ds(mine, 2 * R)], oc.at[pl.ds(mine, 2 * R)], qs_sem.at[1], qr_sem.at[1], (grp, mate))
    q_swap.start()
    o_swap.start()
    q_swap.wait()
    o_swap.wait()
    qt[...] = qc[...].T
    ot[...] = oc[...].T

    def kv_arrived(d):
        remote(kv.at[d], kv.at[d], ks_sem.at[0], kr_sem.at[d], (grp, mate)).wait_recv()

    row_in_block = lax.broadcasted_iota(jnp.int32, (R, R), 0)

    def stats_step(d, carry):
        @pl.when((d == 1) & middle)
        def _():
            kv_arrived(1)
            start_all(own_relay)

        @pl.when((d == 1) & (x >= 1))
        def _():
            kv_arrived(4)
            start_all(near_sends)

        @pl.when((d == 2) & (x >= 1))
        def _():
            kv_arrived(near_slot)
            start_all(near_relay)

        @pl.when((d == 3) & (x >= 2))
        def _():
            kv_arrived(8)
            start_all(next_sends)

        @pl.when((d == 5) & (x >= 2) & middle)
        def _():
            kv_arrived(7)
            start_all(next_relay)

        @pl.when(chip >= d)
        def _():
            @pl.when((d != 0) & jnp.logical_not(early(d)))
            def _():
                kv_arrived(d)

            key_pos = row_in_block + ((chip - d) * 2 + core) * R
            keys = kv[d, :, 0:HD]
            values = kv[d, :, HD:2 * HD]
            for g in range(4):
                sl = slice(g * R, (g + 1) * R)
                s = jnp.dot(keys, qt[:, sl], preferred_element_type=jnp.float32) * SCALE2
                ok = (key_pos >= low[:, sl]) & (key_pos <= high[:, sl])
                s = jnp.where(ok, s, HIDDEN)
                m_old = stat[0:1, sl]
                m_new = jnp.maximum(m_old, jnp.max(s, axis=0, keepdims=True))
                alpha = jnp.exp2(m_old - m_new)
                p = jnp.exp2(s - m_new)
                dp = jnp.dot(values, ot[:, sl], preferred_element_type=jnp.float32)
                stat[0:1, sl] = m_new
                stat[1:2, sl] = stat[1:2, sl] * alpha + jnp.sum(p, axis=0, keepdims=True)
                stat[2:3, sl] = stat[2:3, sl] * alpha + jnp.sum(p * dp, axis=0, keepdims=True)
                mrun[d, :, sl] = m_new
                prob[d, :, sl] = p
                dprob[d, :, sl] = dp

        return carry

    lax.fori_loop(0, 9 + core, stats_step, 0)

    stat_swap = remote(stat, stat_in, ss_sem, sr_sem, (grp, mate))
    stat_swap.start()
    stat_swap.wait()
    m_all = jnp.maximum(stat[0:1, :], stat_in[0:1, :])
    here = jnp.exp2(stat[0:1, :] - m_all)
    there = jnp.exp2(stat_in[0:1, :] - m_all)
    total = stat[1:2, :] * here + stat_in[1:2, :] * there
    weighted = stat[2:3, :] * here + stat_in[2:3, :] * there
    stat[4:5, :] = m_all + jnp.log2(total)
    stat[5:6, :] = weighted / total

    def part_copy(d):
        owner = chip - d
        oy = lax.rem(owner, SIDE)
        a = x - lax.div(owner, SIDE)
        t = lax.rem(oy - y + SIDE, SIDE)
        forward = (t == 1) | ((t == 2) & (a > 0))
        ty = jnp.where((a == 3) | jnp.logical_not(forward), down, up)
        tx = x - 3 * lax.div(a, 3)
        return remote(part.at[d], got.at[4 * a + t], ps_sem.at[d], pr_sem.at[4 * a + t], at(tx, ty))

    def grads_step(i, carry):
        d = 8 + core - i

        @pl.when(chip >= d)
        def _():
            plow, slow = [], []
            for g in range(4):
                sl = slice(g * R, (g + 1) * R)
                factor = jnp.exp2(mrun[d, :, sl] - stat[4:5, sl])
                p = prob[d, :, sl] * factor
                plow.append(p.astype(jnp.bfloat16))
                slow.append((p * (dprob[d, :, sl] - stat[5:6, sl])).astype(jnp.bfloat16))
            keys = kv[d, :, 0:HD]
            for b in range(2):
                dqt[b] += lax.dot_general(
                    keys, jnp.concatenate(slow[2 * b:2 * b + 2], axis=1),
                    (((0,), (0,)), ((), ())), preferred_element_type=jnp.float32,
                )
            dk = jnp.dot(jnp.concatenate(slow, axis=1), qc[...], preferred_element_type=jnp.float32)
            dv = jnp.dot(jnp.concatenate(plow, axis=1), oc[...], preferred_element_type=jnp.float32)

            stays = (d == 0) | early(d)

            @pl.when(stays)
            def _():
                accf[d, :, 0:HD] = dk
                accf[d, :, HD:2 * HD] = dv

            @pl.when(jnp.logical_not(stays))
            def _():
                part[d, :, 0:HD] = dk.astype(jnp.bfloat16)
                part[d, :, HD:2 * HD] = dv.astype(jnp.bfloat16)
                part_copy(d).start()

        return carry

    lax.fori_loop(0, 9 + core, grads_step, 0)

    dq_swap = remote(dqt.at[1 - core], dq_in, ds_sem, dr_sem, (grp, mate))
    dq_swap.start()

    def add(d, slot, cond):
        @pl.when(cond)
        def _():
            remote(got.at[slot], got.at[slot], ps_sem.at[0], pr_sem.at[slot], (grp, mate)).wait_recv()
            accf[d] += got[slot].astype(jnp.float32)

    def pass_on(d, cond, copy):
        @pl.when(cond)
        def _():
            part[d] = accf[d].astype(jnp.bfloat16)
            copy.start()

    def x_copy(d, slot):
        return remote(part.at[d], got.at[slot], ps_sem.at[d], pr_sem.at[slot], at(x_down, y))

    add(7, 10, (x >= 2) & middle)
    pass_on(7, (x >= 2) & middle, part_copy(7))
    add(near_slot, 6, x >= 1)
    pass_on(near_slot, x >= 1, part_copy(near_slot))
    add(8, 9, (x >= 2) & (y >= 1))
    add(8, 11, (x >= 2) & ((y == SIDE - 1) | (core == 1)))
    pass_on(8, x >= 2, x_copy(8, 8))
    add(1, 2, middle)
    pass_on(1, middle, part_copy(1))
    add(4, 7, x >= 1)
    add(4, 5, x >= 1)
    add(4, 8, (x >= 1) & (x < SIDE - 1))
    pass_on(4, x >= 1, x_copy(4, 4))
    add(0, 3, y < SIDE - 1)
    add(0, 1, y == 0)

    dq_swap.wait()
    mixed = dqt[core] + dq_in[...]
    for h in range(2):
        dq_out[:, h * HD:(h + 1) * HD] = (mixed[:, h * R:(h + 1) * R].T * SCALE).astype(jnp.bfloat16)

    add(0, 4, x < SIDE - 1)
    add(0, 15, far_out)

    wide_out = HD // share
    turned = accf[0].T
    for m in range(share):
        for s in range(2):
            piece = turned[s * HD + m * wide_out:s * HD + (m + 1) * wide_out, :]
            zown[m, s * wide_out:(s + 1) * wide_out, :] = piece
            zout[m, s * wide_out:(s + 1) * wide_out, :] = piece.astype(jnp.bfloat16)
    z_sends = []
    for e in range(1, share):
        to = lax.rem(member + e, share)
        z_sends.append(
            remote(zout.at[to], zin.at[member], zs_sem.at[to], zr_sem.at[member], (grp - member + to, srv))
        )
    for copy in z_sends:
        copy.start()
    result = zown[member]
    for e in range(1, share):
        sender = lax.rem(member + e, share)
        remote(zin.at[sender], zin.at[sender], zs_sem.at[0], zr_sem.at[sender], (grp, mate)).wait_recv()
        result = result + zin[sender].astype(jnp.float32)
    dk_out[...] = (result[0:wide_out] * SCALE).astype(jnp.bfloat16)
    dv_out[...] = result[wide_out:2 * wide_out].astype(jnp.bfloat16)

    for sends in (own_sends, own_relay, near_sends, near_relay, next_sends, next_relay):
        for cond, copy in sends:
            pl.when(cond)(copy.wait_send)

    def parts_sent(d, carry):
        @pl.when((chip >= d) & ((d != 4) | (x >= 1)) & ((d != 8) | (x >= 2)))
        def _():
            part_copy(d).wait_send()

        return carry

    lax.fori_loop(1, 9 + core, parts_sent, 0)
    for copy in z_sends:
        copy.wait_send()


def on_device(queries, key_rows, value_rows, grad_output, doc_ids):
    R = queries.shape[0]
    share = lax.axis_size("grp") // (key_rows.shape[1] // HD)
    wide = min(128, R)
    docs = doc_ids.reshape(-1, wide)
    bf, f32, i32 = jnp.bfloat16, jnp.float32, jnp.int32
    dma = pltpu.SemaphoreType.DMA
    scratch = [
        pltpu.VMEM((10, R, 2 * HD), bf),
        pltpu.VMEM((4 * R, HD), bf),
        pltpu.VMEM((4 * R, HD), bf),
        pltpu.VMEM((HD, 4 * R), bf),
        pltpu.VMEM((HD, 4 * R), bf),
        pltpu.VMEM((1, 4 * R), i32),
        pltpu.VMEM((1, 4 * R), i32),
        pltpu.VMEM((10, R, 4 * R), f32),
        pltpu.VMEM((10, R, 4 * R), f32),
        pltpu.VMEM((10, 1, 4 * R), f32),
        pltpu.VMEM((8, 4 * R), f32),
        pltpu.VMEM((8, 4 * R), f32),
        pltpu.VMEM((2, HD, 2 * R), f32),
        pltpu.VMEM((HD, 2 * R), f32),
        pltpu.VMEM((10, R, 2 * HD), bf),
        pltpu.VMEM((16, R, 2 * HD), bf),
        pltpu.VMEM((10, R, 2 * HD), f32),
        pltpu.VMEM((share, 2 * HD // share, R), f32),
        pltpu.VMEM((share, 2 * HD // share, R), bf),
        pltpu.VMEM((share, 2 * HD // share, R), bf),
        dma((6,)), dma((2,)), dma((2,)), dma((13,)), dma((10,)), dma(()), dma(()),
        dma((10,)), dma((16,)), dma((share,)), dma((share,)),
        dma(()), dma(()),
    ]
    vmem = pl.BlockSpec(memory_space=pltpu.VMEM)
    hbm = pl.BlockSpec(memory_space=pltpu.HBM)
    dq, dk, dv = pl.pallas_call(
        functools.partial(kernel, share),
        out_shape=(
            jax.ShapeDtypeStruct((R, 2 * HD), bf),
            jax.ShapeDtypeStruct((HD // share, R), bf),
            jax.ShapeDtypeStruct((HD // share, R), bf),
        ),
        in_specs=[hbm, hbm, hbm, hbm, vmem],
        out_specs=(vmem, vmem, vmem),
        scratch_shapes=scratch,
        compiler_params=pltpu.CompilerParams(
            collective_id=0, has_side_effects=True, vmem_limit_bytes=63 * 1024 * 1024
        ),
    )(queries, key_rows, value_rows, grad_output, docs)
    return dq, dk.T, dv.T


def solution(mesh):
    in_specs = (P("srv", "grp"), P("srv", None), P("srv", None), P("srv", "grp"), P())
    out_specs = (P("srv", "grp"), P("srv", "grp"), P("srv", "grp"))
    return jax.shard_map(
        on_device, mesh=mesh, in_specs=in_specs, out_specs=out_specs, check_vma=False
    )
```

```python
import functools
import math

import jax
import jax.numpy as jnp
from jax import lax
from jax.experimental import pallas as pl
from jax.experimental.pallas import tpu as pltpu
from jax.sharding import PartitionSpec as P

HD = 128
SIDE = 4
SLOTS = 7
HIDDEN = -1e30
MESH = pl.DeviceIdType.MESH
SCALE = HD ** -0.5
SCALE2 = SCALE * math.log2(math.e)


def kernel(
    share, q_ref, k_ref, v_ref, o_ref, doc_ref,
    dq_out, dk_out, dv_out,
    kv, qc, oc, qt, ot, low, high, prob, dprob, mrun, stat, stat_in, norm,
    dqt, dq_in, zq_out, zq_in, part, got, accf, xout, xin, zown, zout, zin, zsum,
    loc_sem, qs_sem, qr_sem, ks_sem, kr_sem, ss_sem, sr_sem, ps_sem, pr_sem,
    xs_sem, xr_sem, zs_sem, zr_sem, ds_sem, dr_sem,
):
    R = q_ref.shape[0]
    grp = lax.axis_index("grp")
    srv = lax.axis_index("srv")
    core = lax.rem(srv, 2)
    chip = lax.div(srv, 2)
    y = lax.rem(chip, SIDE)
    x = lax.div(chip, SIDE)
    member = lax.rem(grp, share)
    kv_head = lax.div(grp, share)
    plane = lax.rem(grp, 2)
    mate = (grp, srv + 1 - 2 * core)
    zmate = (grp + 1 - 2 * plane, srv)
    corner = (grp + 1 - 2 * plane, srv + 1 - 2 * core)
    side = lax.rem(x + y, 2)
    holds = side == plane
    column = lax.div(y, 2)

    def at(cx, cy):
        return (grp, (cx * SIDE + cy) * 2 + core)

    def remote(src, dst, ssem, rsem, device):
        return pltpu.make_async_remote_copy(
            src_ref=src, dst_ref=dst, send_sem=ssem, recv_sem=rsem,
            device_id=device, device_id_type=MESH,
        )

    col = pl.ds(pl.multiple_of(kv_head * HD, HD), HD)
    local_kv = [
        pltpu.make_async_copy(k_ref.at[:, col], kv.at[column, :, pl.ds(0, HD)], loc_sem.at[0]),
        pltpu.make_async_copy(v_ref.at[:, col], kv.at[column, :, pl.ds(HD, HD)], loc_sem.at[1]),
    ]
    local_q = []
    for h in range(2):
        rows = pl.ds(h * R, R)
        cols = pl.ds(h * HD, HD)
        local_q.append(pltpu.make_async_copy(q_ref.at[:, cols], qc.at[rows], loc_sem.at[2 + 2 * h]))
        local_q.append(pltpu.make_async_copy(o_ref.at[:, cols], oc.at[rows], loc_sem.at[3 + 2 * h]))
    for copy in local_kv:
        pl.when(holds)(copy.start)
    for copy in local_q:
        copy.start()

    barrier = pltpu.get_barrier_semaphore()

    def greet(device):
        pl.semaphore_signal(barrier, inc=1, device_id=device, device_id_type=MESH)

    far_out = (chip == 3) & (core == 1) & (plane == 1)
    far_in = (chip == 12) & (core == 1) & (plane == 1)
    greet(mate)
    greet(corner)
    for e in range(1, SIDE):
        greet(at(x, lax.rem(y + e, SIDE)))
        greet(at(lax.rem(x + e, SIDE), y))
    for e in range(1, share):
        greet((grp - member + lax.rem(member + e, share), srv))

    @pl.when(far_out)
    def _():
        greet(at(3, 0))

    @pl.when(far_in)
    def _():
        greet(at(0, 3))

    wide = doc_ref.shape[1]
    number = lax.broadcasted_iota(jnp.int32, (32, wide), 0)
    count = jnp.zeros((32, wide), jnp.int32)
    for r in range(doc_ref.shape[0]):
        count = count + (doc_ref[pl.ds(r, 1), :] < number).astype(jnp.int32)
    first = jnp.sum(count, axis=1, keepdims=True)
    lane = lax.broadcasted_iota(jnp.int32, (1, wide), 1)
    per = R // wide
    for b in range(2):
        block = chip * 2 + (core if b == 0 else 1 - core)
        for t in range(per):
            row = block * per + t
            own = doc_ref[pl.ds(row, 1), :]
            low[b:b + 1, t * wide:(t + 1) * wide] = jnp.sum(
                jnp.where(own == number, first, 0), axis=0, keepdims=True
            )
            high[b:b + 1, t * wide:(t + 1) * wide] = lane + row * wide

    stat[0:8, :] = jnp.full((8, R), HIDDEN, jnp.float32)
    stat[8:24, :] = jnp.zeros((16, R), jnp.float32)
    dqt[...] = jnp.zeros_like(dqt)

    far = jnp.where(far_out | far_in, 1, 0)
    pl.semaphore_wait(barrier, 2 + 2 * (SIDE - 1) + share - 1 + far)

    def swap(n, src, dst, device):
        return [
            remote(ref.at[pl.ds(src * 2 * R, 2 * R)], ref.at[pl.ds(dst * 2 * R, 2 * R)],
                   qs_sem.at[2 * n + i], qr_sem.at[2 * n + i], device)
            for i, ref in enumerate((qc, oc))
        ]

    to_core, to_plane, to_corner = swap(0, 0, 1, mate), swap(1, 0, 2, zmate), swap(2, 2, 3, mate)

    def kv_send(n, src, dst, device):
        return remote(kv.at[src], kv.at[dst], ks_sem.at[n], kr_sem.at[dst], device)

    own_sends, near_sends, next_sends = [], [], []
    for e in range(1, 3):
        own_sends.append(
            (holds & (x + e < SIDE), kv_send(e - 1, column, 2 * e + column, at(lax.rem(x + e, SIDE), y)))
        )
    own_sends.append((far_out, kv_send(2, column, 6, at(3, 0))))
    for e in range(1, SIDE):
        there = at(x, lax.rem(y + e, SIDE))
        wraps = y + e >= SIDE
        own_sends.append((holds & jnp.logical_not(wraps), kv_send(2 + e, column, column, there)))
        near_sends.append(
            (jnp.logical_not(holds) & (x >= 1), kv_send(5 + e, 2 + column, 2 + column, there))
        )
        reaches = wraps | (core == 1) if e == 1 else wraps
        next_sends.append((holds & (x >= 2) & reaches, kv_send(8 + e, 4 + column, 4 + column, there)))

    def start_all(sends):
        for cond, copy in sends:
            pl.when(cond)(copy.start)

    for copy in local_kv:
        pl.when(holds)(copy.wait)
    start_all(own_sends)
    for copy in local_q:
        copy.wait()
    for copy in to_plane + to_core:
        copy.start()
    for copy in to_core:
        copy.wait()
    for b in range(2):
        qt[:, b * 2 * R:(b + 1) * 2 * R] = qc[b * 2 * R:(b + 1) * 2 * R, :].T
        ot[:, b * 2 * R:(b + 1) * 2 * R] = oc[b * 2 * R:(b + 1) * 2 * R, :].T

    def kv_arrived(j):
        remote(kv.at[j], kv.at[j], ks_sem.at[0], kr_sem.at[j], mate).wait_recv()

    def slot(j):
        a = lax.div(j, 2)
        ky = jnp.where(a == 3, SIDE - 1, lax.rem(plane + x + a, 2) + 2 * lax.rem(j, 2))
        d = 4 * a + y - ky
        valid = (x >= a) & (d >= 0) & (d <= 8 + core) & ((a < 3) | (plane == 1))
        return a, ky, d, valid

    row_in_block = lax.broadcasted_iota(jnp.int32, (R, R), 0)

    def stats_block(z, j, d):
        key_pos = row_in_block + ((chip - d) * 2 + core) * R
        keys = kv[j, :, 0:HD]
        values = kv[j, :, HD:2 * HD]
        for g in range(4 * z, 4 * z + 4):
            b = (g // 2) % 2
            sl = slice(g * R, (g + 1) * R)
            s = jnp.dot(keys, qt[:, sl], preferred_element_type=jnp.float32) * SCALE2
            ok = (key_pos >= low[b:b + 1, :]) & (key_pos <= high[b:b + 1, :])
            s = jnp.where(ok, s, HIDDEN)
            m_old = stat[g:g + 1, :]
            m_new = jnp.maximum(m_old, jnp.max(s, axis=0, keepdims=True))
            alpha = jnp.exp2(m_old - m_new)
            p = jnp.exp2(s - m_new)
            dp = jnp.dot(values, ot[:, sl], preferred_element_type=jnp.float32)
            stat[g:g + 1, :] = m_new
            stat[8 + g:9 + g, :] = stat[8 + g:9 + g, :] * alpha + jnp.sum(p, axis=0, keepdims=True)
            stat[16 + g:17 + g, :] = stat[16 + g:17 + g, :] * alpha + jnp.sum(p * dp, axis=0, keepdims=True)
            mrun[j, g:g + 1, :] = m_new
            prob[j, :, sl] = p
            dprob[j, :, sl] = dp

    def stats_step(j, carry):
        @pl.when((j == 1) & (x >= 1) & jnp.logical_not(holds))
        def _():
            kv_arrived(2 + column)
            start_all(near_sends)

        @pl.when((j == 2) & (x >= 2) & holds)
        def _():
            kv_arrived(4 + column)
            start_all(next_sends)

        a, ky, d, valid = slot(j)

        @pl.when(valid)
        def _():
            @pl.when(ky != y)
            def _():
                kv_arrived(j)

            stats_block(0, j, d)

        return carry

    lax.fori_loop(0, SLOTS, stats_step, 0)

    for copy in to_plane:
        copy.wait()
    for copy in to_corner:
        copy.start()
    for copy in to_corner:
        copy.wait()
    for b in range(2, 4):
        qt[:, b * 2 * R:(b + 1) * 2 * R] = qc[b * 2 * R:(b + 1) * 2 * R, :].T
        ot[:, b * 2 * R:(b + 1) * 2 * R] = oc[b * 2 * R:(b + 1) * 2 * R, :].T

    def stats_other(j, carry):
        a, ky, d, valid = slot(j)

        @pl.when(valid)
        def _():
            stats_block(1, j, d)

        return carry

    lax.fori_loop(0, SLOTS, stats_other, 0)

    peers = (mate, zmate, corner)
    swaps = [remote(stat, stat_in.at[i], ss_sem.at[i], sr_sem.at[i], peers[i]) for i in range(3)]
    for copy in swaps:
        copy.start()
    for copy in swaps:
        copy.wait()
    for r in range(4):
        def rows_of(kind, r=r):
            mine = [stat[8 * kind + 2 * r:8 * kind + 2 * r + 2, :]]
            for i in range(3):
                there = 8 * kind + 2 * (r ^ (i + 1))
                mine.append(stat_in[i, there:there + 2, :])
            return mine

        tops = rows_of(0)
        top = jnp.maximum(jnp.maximum(tops[0], tops[1]), jnp.maximum(tops[2], tops[3]))
        factors = [jnp.exp2(t - top) for t in tops]
        total = sum(f * t for f, t in zip(factors, rows_of(1)))
        weighted = sum(f * t for f, t in zip(factors, rows_of(2)))
        norm[2 * r:2 * r + 2, :] = top + jnp.log2(total)
        norm[8 + 2 * r:8 + 2 * r + 2, :] = weighted / total

    def part_copy(j):
        a, ky, d, valid = slot(j)
        tx = x - 3 * lax.div(a, 3)
        return remote(part.at[j], got.at[a, y], ps_sem.at[j], pr_sem.at[a, y], at(tx, ky))

    def grads_step(i, carry):
        j = SLOTS - 1 - i
        a, ky, d, valid = slot(j)

        @pl.when(valid)
        def _():
            plow, slow = [], []
            for g in range(8):
                sl = slice(g * R, (g + 1) * R)
                factor = jnp.exp2(mrun[j, g:g + 1, :] - norm[g:g + 1, :])
                p = prob[j, :, sl] * factor
                plow.append(p.astype(jnp.bfloat16))
                slow.append((p * (dprob[j, :, sl] - norm[8 + g:9 + g, :])).astype(jnp.bfloat16))
            keys = kv[j, :, 0:HD]
            dk = jnp.dot(jnp.concatenate(slow, axis=1), qc[...], preferred_element_type=jnp.float32)
            dv = jnp.dot(jnp.concatenate(plow, axis=1), oc[...], preferred_element_type=jnp.float32)

            @pl.when(ky == y)
            def _():
                accf[a, :, 0:HD] = dk
                accf[a, :, HD:2 * HD] = dv

            @pl.when(ky != y)
            def _():
                part[j, :, 0:HD] = dk.astype(jnp.bfloat16)
                part[j, :, HD:2 * HD] = dv.astype(jnp.bfloat16)
                part_copy(j).start()

            for r in range(4):
                dqt[r] += lax.dot_general(
                    keys, jnp.concatenate(slow[2 * r:2 * r + 2], axis=1),
                    (((0,), (0,)), ((), ())), preferred_element_type=jnp.float32,
                )

        return carry

    lax.fori_loop(0, SLOTS, grads_step, 0)

    dq_swaps = [
        remote(dqt.at[2 * i + 1], dq_in.at[i], ds_sem.at[i], dr_sem.at[i], mate) for i in range(2)
    ]
    for copy in dq_swaps:
        copy.start()
    for copy in dq_swaps:
        copy.wait()
    zq_out[...] = (dqt[2] + dq_in[1]).astype(jnp.bfloat16)
    zq_swap = remote(zq_out, zq_in, ds_sem.at[2], dr_sem.at[2], zmate)
    zq_swap.start()

    def part_arrived(a, sy):
        remote(got.at[a, sy], got.at[a, sy], ps_sem.at[0], pr_sem.at[a, sy], mate).wait_recv()

    def gather_row(a, e, cond):
        sy = lax.rem(y + e, SIDE)

        @pl.when(cond)
        def _():
            part_arrived(a, sy)
            accf[a] += got[a, sy].astype(jnp.float32)

    x_sends = []
    for a in (2, 1):
        here = (x >= a) & (holds if a == 2 else jnp.logical_not(holds))
        for e in range(1, SIDE):
            wraps = y + e >= SIDE
            if a == 1:
                cond = here
            else:
                cond = here & (wraps | (core == 1) if e == 1 else wraps)
            gather_row(a, e, cond)
        copy = remote(xout.at[a - 1], xin.at[a - 1], xs_sem.at[a - 1], xr_sem.at[a - 1], at(lax.rem(x - a + SIDE, SIDE), y))
        x_sends.append((here, copy))

        @pl.when(here)
        def _():
            xout[a - 1] = accf[a].astype(jnp.bfloat16)
            copy.start()

    for e in range(1, SIDE):
        gather_row(0, e, holds & (y + e < SIDE))

    zq_swap.wait()
    mixed = dqt[0] + dq_in[0] + zq_in[...].astype(jnp.float32)
    for h in range(2):
        dq_out[:, h * HD:(h + 1) * HD] = (mixed[:, h * R:(h + 1) * R].T * SCALE).astype(jnp.bfloat16)

    for a in (1, 2):
        @pl.when(holds & (x + a < SIDE))
        def _():
            remote(xin.at[a - 1], xin.at[a - 1], xs_sem.at[0], xr_sem.at[a - 1], mate).wait_recv()
            accf[0] += xin[a - 1].astype(jnp.float32)

    @pl.when(far_out)
    def _():
        part_arrived(3, 0)
        accf[0] += got[3, 0].astype(jnp.float32)

    wide_out = HD // share
    pair = lax.div(member, 2)
    z_sends = []
    for e in range(1, share):
        to = lax.rem(member + e, share)
        z_sends.append(
            remote(zout.at[to], zin.at[pair], zs_sem.at[to], zr_sem.at[pair], (grp - member + to, srv))
        )

    @pl.when(holds)
    def _():
        turned = accf[0].T
        for m in range(share):
            for s in range(2):
                piece = turned[s * HD + m * wide_out:s * HD + (m + 1) * wide_out, :]
                zown[m, s * wide_out:(s + 1) * wide_out, :] = piece
                zout[m, s * wide_out:(s + 1) * wide_out, :] = piece.astype(jnp.bfloat16)
        for copy in z_sends:
            copy.start()
        zsum[...] = zown[member]

    @pl.when(jnp.logical_not(holds))
    def _():
        zsum[...] = jnp.zeros_like(zsum)

    for w in range(share // 2):
        @pl.when(jnp.logical_not(holds & (pair == w)))
        def _():
            remote(zin.at[w], zin.at[w], zs_sem.at[0], zr_sem.at[w], mate).wait_recv()
            zsum[...] += zin[w].astype(jnp.float32)

    dk_out[...] = (zsum[0:wide_out, :] * SCALE).astype(jnp.bfloat16)
    dv_out[...] = zsum[wide_out:2 * wide_out, :].astype(jnp.bfloat16)

    for cond, copy in own_sends + near_sends + next_sends + x_sends:
        pl.when(cond)(copy.wait_send)

    def parts_sent(j, carry):
        a, ky, d, valid = slot(j)

        @pl.when(valid & (ky != y))
        def _():
            part_copy(j).wait_send()

        return carry

    lax.fori_loop(0, SLOTS, parts_sent, 0)
    for copy in z_sends:
        pl.when(holds)(copy.wait_send)


def on_device(queries, key_rows, value_rows, grad_output, doc_ids):
    R = queries.shape[0]
    share = lax.axis_size("grp") // (key_rows.shape[1] // HD)
    wide = min(128, R)
    docs = doc_ids.reshape(-1, wide)
    bf, f32, i32 = jnp.bfloat16, jnp.float32, jnp.int32
    dma = pltpu.SemaphoreType.DMA
    scratch = [
        pltpu.VMEM((SLOTS, R, 2 * HD), bf),
        pltpu.VMEM((8 * R, HD), bf),
        pltpu.VMEM((8 * R, HD), bf),
        pltpu.VMEM((HD, 8 * R), bf),
        pltpu.VMEM((HD, 8 * R), bf),
        pltpu.VMEM((2, R), i32),
        pltpu.VMEM((2, R), i32),
        pltpu.VMEM((SLOTS, R, 8 * R), f32),
        pltpu.VMEM((SLOTS, R, 8 * R), f32),
        pltpu.VMEM((SLOTS, 8, R), f32),
        pltpu.VMEM((24, R), f32),
        pltpu.VMEM((3, 24, R), f32),
        pltpu.VMEM((16, R), f32),
        pltpu.VMEM((4, HD, 2 * R), f32),
        pltpu.VMEM((2, HD, 2 * R), f32),
        pltpu.VMEM((HD, 2 * R), bf),
        pltpu.VMEM((HD, 2 * R), bf),
        pltpu.VMEM((SLOTS, R, 2 * HD), bf),
        pltpu.VMEM((4, SIDE, R, 2 * HD), bf),
        pltpu.VMEM((3, R, 2 * HD), f32),
        pltpu.VMEM((2, R, 2 * HD), bf),
        pltpu.VMEM((2, R, 2 * HD), bf),
        pltpu.VMEM((share, 2 * HD // share, R), f32),
        pltpu.VMEM((share, 2 * HD // share, R), bf),
        pltpu.VMEM((share // 2, 2 * HD // share, R), bf),
        pltpu.VMEM((2 * HD // share, R), f32),
        dma((6,)), dma((6,)), dma((6,)), dma((12,)), dma((SLOTS,)), dma((3,)), dma((3,)),
        dma((SLOTS,)), dma((4, SIDE)), dma((2,)), dma((2,)), dma((share,)), dma((share // 2,)),
        dma((3,)), dma((3,)),
    ]
    vmem = pl.BlockSpec(memory_space=pltpu.VMEM)
    hbm = pl.BlockSpec(memory_space=pltpu.HBM)
    dq, dk, dv = pl.pallas_call(
        functools.partial(kernel, share),
        out_shape=(
            jax.ShapeDtypeStruct((R, 2 * HD), bf),
            jax.ShapeDtypeStruct((HD // share, R), bf),
            jax.ShapeDtypeStruct((HD // share, R), bf),
        ),
        in_specs=[hbm, hbm, hbm, hbm, vmem],
        out_specs=(vmem, vmem, vmem),
        scratch_shapes=scratch,
        compiler_params=pltpu.CompilerParams(
            collective_id=0, has_side_effects=True, vmem_limit_bytes=63 * 1024 * 1024
        ),
    )(queries, key_rows, value_rows, grad_output, docs)
    return dq, dk.T, dv.T


def solution(mesh):
    in_specs = (P("srv", "grp"), P("srv", None), P("srv", None), P("srv", "grp"), P())
    out_specs = (P("srv", "grp"), P("srv", "grp"), P("srv", "grp"))
    return jax.shard_map(
        on_device, mesh=mesh, in_specs=in_specs, out_specs=out_specs, check_vma=False
    )
```

```python
import functools
import math

import jax
import jax.numpy as jnp
from jax import lax
from jax.experimental import pallas as pl
from jax.experimental.pallas import tpu as pltpu
from jax.sharding import PartitionSpec as P

HD = 128
SIDE = 4
SLOTS = 7
HIDDEN = -1e30
MESH = pl.DeviceIdType.MESH
SCALE = HD ** -0.5
SCALE2 = SCALE * math.log2(math.e)


def kernel(
    share, q_ref, k_ref, v_ref, o_ref, doc_hbm,
    dq_out, dk_out, dv_out,
    doc_ref, kv, qc, oc, qt, ot, low, high, prob, dprob, mrun, stat, stat_in, norm,
    dqt, dq_in, zq_out, zq_in, part, got, accf, xout, xin, zown, zout, zin, zsum,
    loc_sem, qs_sem, qr_sem, ks_sem, kr_sem, ss_sem, sr_sem, ps_sem, pr_sem,
    xs_sem, xr_sem, zs_sem, zr_sem, ds_sem, dr_sem,
):
    R = q_ref.shape[0]
    grp = lax.axis_index("grp")
    srv = lax.axis_index("srv")
    core = lax.rem(srv, 2)
    chip = lax.div(srv, 2)
    y = lax.rem(chip, SIDE)
    x = lax.div(chip, SIDE)
    member = lax.rem(grp, share)
    kv_head = lax.div(grp, share)
    plane = lax.rem(grp, 2)
    mate = (grp, srv + 1 - 2 * core)
    zmate = (grp + 1 - 2 * plane, srv)
    corner = (grp + 1 - 2 * plane, srv + 1 - 2 * core)
    side = lax.rem(x + y, 2)
    holds = side == plane
    column = lax.div(y, 2)

    def at(cx, cy):
        return (grp, (cx * SIDE + cy) * 2 + core)

    def remote(src, dst, ssem, rsem, device):
        return pltpu.make_async_remote_copy(
            src_ref=src, dst_ref=dst, send_sem=ssem, recv_sem=rsem,
            device_id=device, device_id_type=MESH,
        )

    col = pl.ds(pl.multiple_of(kv_head * HD, HD), HD)
    local_kv = [
        pltpu.make_async_copy(k_ref.at[:, col], kv.at[column, :, pl.ds(0, HD)], loc_sem.at[0]),
        pltpu.make_async_copy(v_ref.at[:, col], kv.at[column, :, pl.ds(HD, HD)], loc_sem.at[1]),
    ]
    local_q = []
    for h in range(2):
        rows = pl.ds(h * R, R)
        cols = pl.ds(h * HD, HD)
        local_q.append(pltpu.make_async_copy(q_ref.at[:, cols], qc.at[rows], loc_sem.at[2 + 2 * h]))
        local_q.append(pltpu.make_async_copy(o_ref.at[:, cols], oc.at[rows], loc_sem.at[3 + 2 * h]))
    local_doc = pltpu.make_async_copy(doc_hbm, doc_ref, loc_sem.at[6])
    local_doc.start()
    for copy in local_kv:
        pl.when(holds)(copy.start)
    for copy in local_q:
        copy.start()

    barrier = pltpu.get_barrier_semaphore()

    def greet(device):
        pl.semaphore_signal(barrier, inc=1, device_id=device, device_id_type=MESH)

    far_out = (chip == 3) & (core == 1) & (plane == 1)
    far_in = (chip == 12) & (core == 1) & (plane == 1)
    greet(mate)
    greet(corner)
    for e in range(1, SIDE):
        greet(at(x, lax.rem(y + e, SIDE)))
        greet(at(lax.rem(x + e, SIDE), y))
    for e in range(1, share):
        greet((grp - member + lax.rem(member + e, share), srv))

    @pl.when(far_out)
    def _():
        greet(at(3, 0))

    @pl.when(far_in)
    def _():
        greet(at(0, 3))

    local_doc.wait()
    wide = doc_ref.shape[1]
    number = lax.broadcasted_iota(jnp.int32, (32, wide), 0)
    count = jnp.zeros((32, wide), jnp.int32)
    for r in range(doc_ref.shape[0]):
        count = count + (doc_ref[pl.ds(r, 1), :] < number).astype(jnp.int32)
    first = jnp.sum(count, axis=1, keepdims=True)
    lane = lax.broadcasted_iota(jnp.int32, (1, wide), 1)
    per = R // wide
    for b in range(2):
        block = chip * 2 + (core if b == 0 else 1 - core)
        for t in range(per):
            row = block * per + t
            own = doc_ref[pl.ds(row, 1), :]
            low[b:b + 1, t * wide:(t + 1) * wide] = jnp.sum(
                jnp.where(own == number, first, 0), axis=0, keepdims=True
            )
            high[b:b + 1, t * wide:(t + 1) * wide] = lane + row * wide

    stat[0:8, :] = jnp.full((8, R), HIDDEN, jnp.float32)
    stat[8:24, :] = jnp.zeros((16, R), jnp.float32)
    dqt[...] = jnp.zeros_like(dqt)

    far = jnp.where(far_out | far_in, 1, 0)
    pl.semaphore_wait(barrier, 2 + 2 * (SIDE - 1) + share - 1 + far)

    def swap(n, src, dst, device):
        return [
            remote(ref.at[pl.ds(src * 2 * R, 2 * R)], ref.at[pl.ds(dst * 2 * R, 2 * R)],
                   qs_sem.at[2 * n + i], qr_sem.at[2 * n + i], device)
            for i, ref in enumerate((qc, oc))
        ]

    to_core, to_plane, to_corner = swap(0, 0, 1, mate), swap(1, 0, 2, zmate), swap(2, 2, 3, mate)

    def kv_send(n, src, dst, device):
        return remote(kv.at[src], kv.at[dst], ks_sem.at[n], kr_sem.at[dst], device)

    own_sends, near_sends, next_sends = [], [], []
    for e in range(1, 3):
        own_sends.append(
            (holds & (x + e < SIDE), kv_send(e - 1, column, 2 * e + column, at(lax.rem(x + e, SIDE), y)))
        )
    own_sends.append((far_out, kv_send(2, column, 6, at(3, 0))))
    for e in range(1, SIDE):
        there = at(x, lax.rem(y + e, SIDE))
        wraps = y + e >= SIDE
        own_sends.append((holds & jnp.logical_not(wraps), kv_send(2 + e, column, column, there)))
        near_sends.append(
            (jnp.logical_not(holds) & (x >= 1), kv_send(5 + e, 2 + column, 2 + column, there))
        )
        reaches = wraps | (core == 1) if e == 1 else wraps
        next_sends.append((holds & (x >= 2) & reaches, kv_send(8 + e, 4 + column, 4 + column, there)))

    def start_all(sends):
        for cond, copy in sends:
            pl.when(cond)(copy.start)

    for copy in local_kv:
        pl.when(holds)(copy.wait)
    start_all(own_sends)
    for copy in local_q:
        copy.wait()
    for copy in to_plane + to_core:
        copy.start()
    for copy in to_core:
        copy.wait()
    for b in range(2):
        qt[:, b * 2 * R:(b + 1) * 2 * R] = qc[b * 2 * R:(b + 1) * 2 * R, :].T
        ot[:, b * 2 * R:(b + 1) * 2 * R] = oc[b * 2 * R:(b + 1) * 2 * R, :].T

    def kv_arrived(j):
        remote(kv.at[j], kv.at[j], ks_sem.at[0], kr_sem.at[j], mate).wait_recv()

    def slot(j):
        a = lax.div(j, 2)
        ky = jnp.where(a == 3, SIDE - 1, lax.rem(plane + x + a, 2) + 2 * lax.rem(j, 2))
        d = 4 * a + y - ky
        valid = (x >= a) & (d >= 0) & (d <= 8 + core) & ((a < 3) | (plane == 1))
        return a, ky, d, valid

    row_in_block = lax.broadcasted_iota(jnp.int32, (R, R), 0)

    def stats_block(z, j, d):
        key_pos = row_in_block + ((chip - d) * 2 + core) * R
        keys = kv[j, :, 0:HD]
        values = kv[j, :, HD:2 * HD]
        for g in range(4 * z, 4 * z + 4):
            b = (g // 2) % 2
            sl = slice(g * R, (g + 1) * R)
            s = jnp.dot(keys, qt[:, sl], preferred_element_type=jnp.float32) * SCALE2
            ok = (key_pos >= low[b:b + 1, :]) & (key_pos <= high[b:b + 1, :])
            s = jnp.where(ok, s, HIDDEN)
            m_old = stat[g:g + 1, :]
            m_new = jnp.maximum(m_old, jnp.max(s, axis=0, keepdims=True))
            alpha = jnp.exp2(m_old - m_new)
            p = jnp.exp2(s - m_new)
            dp = jnp.dot(values, ot[:, sl], preferred_element_type=jnp.float32)
            stat[g:g + 1, :] = m_new
            stat[8 + g:9 + g, :] = stat[8 + g:9 + g, :] * alpha + jnp.sum(p, axis=0, keepdims=True)
            stat[16 + g:17 + g, :] = stat[16 + g:17 + g, :] * alpha + jnp.sum(p * dp, axis=0, keepdims=True)
            mrun[j, g:g + 1, :] = m_new
            prob[j, :, sl] = p
            dprob[j, :, sl] = dp

    def stats_step(j, carry):
        @pl.when((j == 1) & (x >= 1) & jnp.logical_not(holds))
        def _():
            kv_arrived(2 + column)
            start_all(near_sends)

        @pl.when((j == 2) & (x >= 2) & holds)
        def _():
            kv_arrived(4 + column)
            start_all(next_sends)

        @pl.when(j == 4)
        def _():
            for copy in to_plane:
                copy.wait()
            for copy in to_corner:
                copy.start()

        a, ky, d, valid = slot(j)

        @pl.when(valid)
        def _():
            @pl.when(ky != y)
            def _():
                kv_arrived(j)

            stats_block(0, j, d)

        return carry

    lax.fori_loop(0, SLOTS, stats_step, 0)

    for copy in to_corner:
        copy.wait()
    for b in range(2, 4):
        qt[:, b * 2 * R:(b + 1) * 2 * R] = qc[b * 2 * R:(b + 1) * 2 * R, :].T
        ot[:, b * 2 * R:(b + 1) * 2 * R] = oc[b * 2 * R:(b + 1) * 2 * R, :].T

    def stats_other(j, carry):
        a, ky, d, valid = slot(j)

        @pl.when(valid)
        def _():
            stats_block(1, j, d)

        return carry

    lax.fori_loop(0, SLOTS, stats_other, 0)

    peers = (mate, zmate, corner)
    swaps = [remote(stat, stat_in.at[i], ss_sem.at[i], sr_sem.at[i], peers[i]) for i in range(3)]
    for copy in swaps:
        copy.start()
    for copy in swaps:
        copy.wait()
    for r in range(4):
        def rows_of(kind, r=r):
            mine = [stat[8 * kind + 2 * r:8 * kind + 2 * r + 2, :]]
            for i in range(3):
                there = 8 * kind + 2 * (r ^ (i + 1))
                mine.append(stat_in[i, there:there + 2, :])
            return mine

        tops = rows_of(0)
        top = jnp.maximum(jnp.maximum(tops[0], tops[1]), jnp.maximum(tops[2], tops[3]))
        factors = [jnp.exp2(t - top) for t in tops]
        total = sum(f * t for f, t in zip(factors, rows_of(1)))
        weighted = sum(f * t for f, t in zip(factors, rows_of(2)))
        norm[2 * r:2 * r + 2, :] = top + jnp.log2(total)
        norm[8 + 2 * r:8 + 2 * r + 2, :] = weighted / total

    def part_copy(j):
        a, ky, d, valid = slot(j)
        tx = x - 3 * lax.div(a, 3)
        return remote(part.at[j], got.at[a, y], ps_sem.at[j], pr_sem.at[a, y], at(tx, ky))

    def part_arrived(a, sy):
        remote(got.at[a, sy], got.at[a, sy], ps_sem.at[0], pr_sem.at[a, sy], mate).wait_recv()

    def gather_row(a, e, cond):
        sy = lax.rem(y + e, SIDE)

        @pl.when(cond)
        def _():
            part_arrived(a, sy)
            accf[a] += got[a, sy].astype(jnp.float32)

    def x_hand_over(a):
        for e in range(1, SIDE):
            wraps = y + e >= SIDE
            reaches = True if a == 1 else (wraps | (core == 1) if e == 1 else wraps)
            gather_row(a, e, x_here[a] & reaches)

        @pl.when(x_here[a])
        def _():
            xout[a - 1] = accf[a].astype(jnp.bfloat16)
            x_copy[a].start()

    x_here = {1: (x >= 1) & jnp.logical_not(holds), 2: (x >= 2) & holds}
    x_copy = {
        a: remote(xout.at[a - 1], xin.at[a - 1], xs_sem.at[a - 1], xr_sem.at[a - 1],
                  at(lax.rem(x - a + SIDE, SIDE), y))
        for a in (1, 2)
    }

    def grads_step(i, carry):
        j = SLOTS - 1 - i
        a, ky, d, valid = slot(j)

        @pl.when(j == 1)
        def _():
            x_hand_over(2)

        @pl.when(valid)
        def _():
            plow, slow = [], []
            for g in range(8):
                sl = slice(g * R, (g + 1) * R)
                factor = jnp.exp2(mrun[j, g:g + 1, :] - norm[g:g + 1, :])
                p = prob[j, :, sl] * factor
                plow.append(p.astype(jnp.bfloat16))
                slow.append((p * (dprob[j, :, sl] - norm[8 + g:9 + g, :])).astype(jnp.bfloat16))
            keys = kv[j, :, 0:HD]
            dk = jnp.dot(jnp.concatenate(slow, axis=1), qc[...], preferred_element_type=jnp.float32)
            dv = jnp.dot(jnp.concatenate(plow, axis=1), oc[...], preferred_element_type=jnp.float32)

            @pl.when(ky == y)
            def _():
                accf[a, :, 0:HD] = dk
                accf[a, :, HD:2 * HD] = dv

            @pl.when(ky != y)
            def _():
                part[j, :, 0:HD] = dk.astype(jnp.bfloat16)
                part[j, :, HD:2 * HD] = dv.astype(jnp.bfloat16)
                part_copy(j).start()

            for r in range(4):
                dqt[r] += lax.dot_general(
                    keys, jnp.concatenate(slow[2 * r:2 * r + 2], axis=1),
                    (((0,), (0,)), ((), ())), preferred_element_type=jnp.float32,
                )

        return carry

    lax.fori_loop(0, SLOTS, grads_step, 0)

    dq_swaps = [
        remote(dqt.at[2 * i + 1], dq_in.at[i], ds_sem.at[i], dr_sem.at[i], mate) for i in range(2)
    ]
    for copy in dq_swaps:
        copy.start()

    x_hand_over(1)
    for copy in dq_swaps:
        copy.wait()
    zq_out[...] = (dqt[2] + dq_in[1]).astype(jnp.bfloat16)
    zq_swap = remote(zq_out, zq_in, ds_sem.at[2], dr_sem.at[2], zmate)
    zq_swap.start()

    for e in range(1, SIDE):
        gather_row(0, e, holds & (y + e < SIDE))

    for a in (1, 2):
        @pl.when(holds & (x + a < SIDE))
        def _():
            remote(xin.at[a - 1], xin.at[a - 1], xs_sem.at[0], xr_sem.at[a - 1], mate).wait_recv()
            accf[0] += xin[a - 1].astype(jnp.float32)

    @pl.when(far_out)
    def _():
        part_arrived(3, 0)
        accf[0] += got[3, 0].astype(jnp.float32)

    wide_out = HD // share
    pair = lax.div(member, 2)
    z_sends = []
    for e in range(1, share):
        to = lax.rem(member + e, share)
        z_sends.append(
            remote(zout.at[to], zin.at[pair], zs_sem.at[to], zr_sem.at[pair], (grp - member + to, srv))
        )

    @pl.when(holds)
    def _():
        turned = accf[0].T
        for m in range(share):
            for s in range(2):
                piece = turned[s * HD + m * wide_out:s * HD + (m + 1) * wide_out, :]
                zown[m, s * wide_out:(s + 1) * wide_out, :] = piece
                zout[m, s * wide_out:(s + 1) * wide_out, :] = piece.astype(jnp.bfloat16)
        for copy in z_sends:
            copy.start()
        zsum[...] = zown[member]

    @pl.when(jnp.logical_not(holds))
    def _():
        zsum[...] = jnp.zeros_like(zsum)

    zq_swap.wait()
    mixed = dqt[0] + dq_in[0] + zq_in[...].astype(jnp.float32)
    for h in range(2):
        dq_out[:, h * HD:(h + 1) * HD] = (mixed[:, h * R:(h + 1) * R].T * SCALE).astype(jnp.bfloat16)

    for w in range(share // 2):
        @pl.when(jnp.logical_not(holds & (pair == w)))
        def _():
            remote(zin.at[w], zin.at[w], zs_sem.at[0], zr_sem.at[w], mate).wait_recv()
            zsum[...] += zin[w].astype(jnp.float32)

    dk_out[...] = (zsum[0:wide_out, :] * SCALE).astype(jnp.bfloat16)
    dv_out[...] = zsum[wide_out:2 * wide_out, :].astype(jnp.bfloat16)

    for cond, copy in own_sends + near_sends + next_sends + [(x_here[a], x_copy[a]) for a in (1, 2)]:
        pl.when(cond)(copy.wait_send)

    def parts_sent(j, carry):
        a, ky, d, valid = slot(j)

        @pl.when(valid & (ky != y))
        def _():
            part_copy(j).wait_send()

        return carry

    lax.fori_loop(0, SLOTS, parts_sent, 0)
    for copy in z_sends:
        pl.when(holds)(copy.wait_send)


def write_out(a_ref, b_ref, c_ref, a_out, b_out, c_out, sem):
    copies = [
        pltpu.make_async_copy(src, dst, sem.at[i])
        for i, (src, dst) in enumerate(((a_ref, a_out), (b_ref, b_out), (c_ref, c_out)))
    ]
    for copy in copies:
        copy.start()
    for copy in copies:
        copy.wait()


def on_device(queries, key_rows, value_rows, grad_output, doc_ids):
    R = queries.shape[0]
    share = lax.axis_size("grp") // (key_rows.shape[1] // HD)
    wide = min(128, R)
    docs = doc_ids.reshape(-1, wide)
    bf, f32, i32 = jnp.bfloat16, jnp.float32, jnp.int32
    dma = pltpu.SemaphoreType.DMA
    scratch = [
        pltpu.VMEM(docs.shape, i32),
        pltpu.VMEM((SLOTS, R, 2 * HD), bf),
        pltpu.VMEM((8 * R, HD), bf),
        pltpu.VMEM((8 * R, HD), bf),
        pltpu.VMEM((HD, 8 * R), bf),
        pltpu.VMEM((HD, 8 * R), bf),
        pltpu.VMEM((2, R), i32),
        pltpu.VMEM((2, R), i32),
        pltpu.VMEM((SLOTS, R, 8 * R), f32),
        pltpu.VMEM((SLOTS, R, 8 * R), f32),
        pltpu.VMEM((SLOTS, 8, R), f32),
        pltpu.VMEM((24, R), f32),
        pltpu.VMEM((3, 24, R), f32),
        pltpu.VMEM((16, R), f32),
        pltpu.VMEM((4, HD, 2 * R), f32),
        pltpu.VMEM((2, HD, 2 * R), f32),
        pltpu.VMEM((HD, 2 * R), bf),
        pltpu.VMEM((HD, 2 * R), bf),
        pltpu.VMEM((SLOTS, R, 2 * HD), bf),
        pltpu.VMEM((4, SIDE, R, 2 * HD), bf),
        pltpu.VMEM((3, R, 2 * HD), f32),
        pltpu.VMEM((2, R, 2 * HD), bf),
        pltpu.VMEM((2, R, 2 * HD), bf),
        pltpu.VMEM((share, 2 * HD // share, R), f32),
        pltpu.VMEM((share, 2 * HD // share, R), bf),
        pltpu.VMEM((share // 2, 2 * HD // share, R), bf),
        pltpu.VMEM((2 * HD // share, R), f32),
        dma((7,)), dma((6,)), dma((6,)), dma((12,)), dma((SLOTS,)), dma((3,)), dma((3,)),
        dma((SLOTS,)), dma((4, SIDE)), dma((2,)), dma((2,)), dma((share,)), dma((share // 2,)),
        dma((3,)), dma((3,)),
    ]
    vmem = pl.BlockSpec(memory_space=pltpu.VMEM)
    hbm = pl.BlockSpec(memory_space=pltpu.HBM)
    dq, dk, dv = pl.pallas_call(
        functools.partial(kernel, share),
        out_shape=(
            pltpu.VMEM((R, 2 * HD), bf),
            pltpu.VMEM((HD // share, R), bf),
            pltpu.VMEM((HD // share, R), bf),
        ),
        in_specs=[hbm, hbm, hbm, hbm, hbm],
        out_specs=(vmem, vmem, vmem),
        scratch_shapes=scratch,
        compiler_params=pltpu.CompilerParams(
            collective_id=0, has_side_effects=True, vmem_limit_bytes=56 * 1024 * 1024
        ),
    )(*(pltpu.with_memory_space_constraint(t, pltpu.HBM) for t in (queries, key_rows, value_rows, grad_output, docs)))
    dq, dk, dv = pl.pallas_call(
        write_out,
        out_shape=tuple(jax.ShapeDtypeStruct(part.shape, part.dtype) for part in (dq, dk, dv)),
        in_specs=[vmem, vmem, vmem],
        out_specs=(hbm, hbm, hbm),
        scratch_shapes=[dma((3,))],
    )(*(pltpu.with_memory_space_constraint(t, pltpu.VMEM) for t in (dq, dk, dv)))
    return dq, dk.T, dv.T


def solution(mesh):
    in_specs = (P("srv", "grp"), P("srv", None), P("srv", None), P("srv", "grp"), P())
    out_specs = (P("srv", "grp"), P("srv", "grp"), P("srv", "grp"))
    return jax.shard_map(
        on_device, mesh=mesh, in_specs=in_specs, out_specs=out_specs, check_vma=False
    )
```

```python
import functools
import math

import jax
import jax.numpy as jnp
from jax import lax
from jax.experimental import pallas as pl
from jax.experimental.pallas import tpu as pltpu
from jax.sharding import PartitionSpec as P

HD = 128
SIDE = 4
SLOTS = 7
HIDDEN = -1e30
MESH = pl.DeviceIdType.MESH
SCALE = HD ** -0.5
SCALE2 = SCALE * math.log2(math.e)


def kernel(
    share, q_ref, k_ref, v_ref, o_ref, doc_hbm,
    dq_out, dk_out, dv_out,
    doc_ref, kv, qc, oc, qt, ot, low, high, prob, dprob, mrun, stat, stat_in, norm,
    dqt, dq_in, zq_out, zq_in, part, got, accf, xout, xin, zown, zout, zin, zsum,
    loc_sem, qs_sem, qr_sem, ks_sem, kr_sem, ss_sem, sr_sem, ps_sem, pr_sem,
    xs_sem, xr_sem, zs_sem, zr_sem, ds_sem, dr_sem, in_sem,
):
    R = q_ref.shape[0]
    grp = lax.axis_index("grp")
    srv = lax.axis_index("srv")
    core = lax.rem(srv, 2)
    chip = lax.div(srv, 2)
    y = lax.rem(chip, SIDE)
    x = lax.div(chip, SIDE)
    member = lax.rem(grp, share)
    kv_head = lax.div(grp, share)
    plane = lax.rem(grp, 2)
    mate = (grp, srv + 1 - 2 * core)
    zmate = (grp + 1 - 2 * plane, srv)
    corner = (grp + 1 - 2 * plane, srv + 1 - 2 * core)
    side = lax.rem(x + y, 2)
    holds = side == plane
    column = lax.div(y, 2)

    def at(cx, cy):
        return (grp, (cx * SIDE + cy) * 2 + core)

    def remote(src, dst, ssem, rsem, device):
        return pltpu.make_async_remote_copy(
            src_ref=src, dst_ref=dst, send_sem=ssem, recv_sem=rsem,
            device_id=device, device_id_type=MESH,
        )

    col = pl.ds(pl.multiple_of(kv_head * HD, HD), HD)
    local_kv = [
        pltpu.make_async_copy(k_ref.at[:, col], kv.at[column, :, pl.ds(0, HD)], loc_sem.at[0]),
        pltpu.make_async_copy(v_ref.at[:, col], kv.at[column, :, pl.ds(HD, HD)], loc_sem.at[1]),
    ]
    local_q = []
    for h in range(2):
        rows = pl.ds(h * R, R)
        cols = pl.ds(h * HD, HD)
        local_q.append(pltpu.make_async_copy(q_ref.at[:, cols], qc.at[rows], loc_sem.at[2 + 2 * h]))
        local_q.append(pltpu.make_async_copy(o_ref.at[:, cols], oc.at[rows], loc_sem.at[3 + 2 * h]))
    local_doc = pltpu.make_async_copy(doc_hbm, doc_ref, loc_sem.at[6])
    local_doc.start()
    for copy in local_kv:
        pl.when(holds)(copy.start)
    for copy in local_q:
        copy.start()

    barrier = pltpu.get_barrier_semaphore()

    def greet(device):
        pl.semaphore_signal(barrier, inc=1, device_id=device, device_id_type=MESH)

    far_out = (chip == 3) & (core == 1) & (plane == 1)
    far_in = (chip == 12) & (core == 1) & (plane == 1)
    everyone = [mate, corner]
    for e in range(1, SIDE):
        everyone += [at(x, lax.rem(y + e, SIDE)), at(lax.rem(x + e, SIDE), y)]
    for e in range(1, share):
        everyone.append((grp - member + lax.rem(member + e, share), srv))

    leader = (member == 0) & (srv == 0)
    beside = ((member == 0) & (srv == 1)) | ((member == 1) & (srv == 0))
    around = (
        ((member == 0) & (core == 0) & (chip > 0) & ((x == 0) | (y == 0)))
        | ((member == 1) & (srv == 1)) | ((member >= 2) & (srv == 0))
    )

    @pl.when(jnp.logical_not(leader))
    def _():
        for device in everyone:
            greet(device)

    @pl.when(far_out)
    def _():
        greet(at(3, 0))

    @pl.when(far_in)
    def _():
        greet(at(0, 3))

    local_doc.wait()
    wide = doc_ref.shape[1]
    number = lax.broadcasted_iota(jnp.int32, (32, wide), 0)
    count = jnp.zeros((32, wide), jnp.int32)
    for r in range(doc_ref.shape[0]):
        count = count + (doc_ref[pl.ds(r, 1), :] < number).astype(jnp.int32)
    first = jnp.sum(count, axis=1, keepdims=True)
    lane = lax.broadcasted_iota(jnp.int32, (1, wide), 1)
    per = R // wide
    for b in range(2):
        block = chip * 2 + (core if b == 0 else 1 - core)
        for t in range(per):
            row = block * per + t
            own = doc_ref[pl.ds(row, 1), :]
            low[b:b + 1, t * wide:(t + 1) * wide] = jnp.sum(
                jnp.where(own == number, first, 0), axis=0, keepdims=True
            )
            high[b:b + 1, t * wide:(t + 1) * wide] = lane + row * wide

    stat[0:8, :] = jnp.full((8, R), HIDDEN, jnp.float32)
    stat[8:24, :] = jnp.zeros((16, R), jnp.float32)
    dqt[...] = jnp.zeros_like(dqt)

    far = jnp.where(far_out | far_in, 1, 0)
    pl.semaphore_wait(barrier, 2 + 2 * (SIDE - 1) + share - 1 + far - jnp.where(beside | around, 1, 0))

    @pl.when(leader)
    def _():
        for device in everyone:
            pl.semaphore_signal(in_sem, inc=1, device_id=device, device_id_type=MESH)

    def swap(n, src, dst, device):
        return [
            remote(ref.at[pl.ds(src * 2 * R, 2 * R)], ref.at[pl.ds(dst * 2 * R, 2 * R)],
                   qs_sem.at[2 * n + i], qr_sem.at[2 * n + i], device)
            for i, ref in enumerate((qc, oc))
        ]

    to_core, to_plane, to_corner = swap(0, 0, 1, mate), swap(1, 0, 2, zmate), swap(2, 2, 3, mate)

    def kv_send(n, src, dst, device):
        return remote(kv.at[src], kv.at[dst], ks_sem.at[n], kr_sem.at[dst], device)

    own_sends, near_sends, next_sends = [], [], []
    for e in range(1, 3):
        own_sends.append(
            (holds & (x + e < SIDE), kv_send(e - 1, column, 2 * e + column, at(lax.rem(x + e, SIDE), y)))
        )
    own_sends.append((far_out, kv_send(2, column, 6, at(3, 0))))
    for e in range(1, SIDE):
        there = at(x, lax.rem(y + e, SIDE))
        wraps = y + e >= SIDE
        own_sends.append((holds & jnp.logical_not(wraps), kv_send(2 + e, column, column, there)))
        near_sends.append(
            (jnp.logical_not(holds) & (x >= 1), kv_send(5 + e, 2 + column, 2 + column, there))
        )
        reaches = wraps | (core == 1) if e == 1 else wraps
        next_sends.append((holds & (x >= 2) & reaches, kv_send(8 + e, 4 + column, 4 + column, there)))

    def start_all(sends):
        for cond, copy in sends:
            pl.when(cond)(copy.start)

    for copy in local_kv:
        pl.when(holds)(copy.wait)
    start_all(own_sends)
    for copy in local_q:
        copy.wait()

    @pl.when(beside)
    def _():
        pl.semaphore_wait(in_sem, 1)

    for copy in to_plane + to_core:
        copy.start()
    for copy in to_core:
        copy.wait()
    for b in range(2):
        qt[:, b * 2 * R:(b + 1) * 2 * R] = qc[b * 2 * R:(b + 1) * 2 * R, :].T
        ot[:, b * 2 * R:(b + 1) * 2 * R] = oc[b * 2 * R:(b + 1) * 2 * R, :].T

    def kv_arrived(j):
        remote(kv.at[j], kv.at[j], ks_sem.at[0], kr_sem.at[j], mate).wait_recv()

    def slot(j):
        a = lax.div(j, 2)
        ky = jnp.where(a == 3, SIDE - 1, lax.rem(plane + x + a, 2) + 2 * lax.rem(j, 2))
        d = 4 * a + y - ky
        valid = (x >= a) & (d >= 0) & (d <= 8 + core) & ((a < 3) | (plane == 1))
        return a, ky, d, valid

    row_in_block = lax.broadcasted_iota(jnp.int32, (R, R), 0)

    def stats_block(z, j, d):
        key_pos = row_in_block + ((chip - d) * 2 + core) * R
        keys = kv[j, :, 0:HD]
        values = kv[j, :, HD:2 * HD]
        for g in range(4 * z, 4 * z + 4):
            b = (g // 2) % 2
            sl = slice(g * R, (g + 1) * R)
            s = jnp.dot(keys, qt[:, sl], preferred_element_type=jnp.float32) * SCALE2
            ok = (key_pos >= low[b:b + 1, :]) & (key_pos <= high[b:b + 1, :])
            s = jnp.where(ok, s, HIDDEN)
            m_old = stat[g:g + 1, :]
            m_new = jnp.maximum(m_old, jnp.max(s, axis=0, keepdims=True))
            alpha = jnp.exp2(m_old - m_new)
            p = jnp.exp2(s - m_new)
            dp = jnp.dot(values, ot[:, sl], preferred_element_type=jnp.float32)
            stat[g:g + 1, :] = m_new
            stat[8 + g:9 + g, :] = stat[8 + g:9 + g, :] * alpha + jnp.sum(p, axis=0, keepdims=True)
            stat[16 + g:17 + g, :] = stat[16 + g:17 + g, :] * alpha + jnp.sum(p * dp, axis=0, keepdims=True)
            mrun[j, g:g + 1, :] = m_new
            prob[j, :, sl] = p
            dprob[j, :, sl] = dp

    def stats_step(j, carry):
        @pl.when((j == 1) & (x >= 1) & jnp.logical_not(holds))
        def _():
            kv_arrived(2 + column)
            start_all(near_sends)

        @pl.when((j == 2) & (x >= 2) & holds)
        def _():
            kv_arrived(4 + column)
            start_all(next_sends)

        @pl.when(j == 4)
        def _():
            for copy in to_plane:
                copy.wait()
            for copy in to_corner:
                copy.start()

        a, ky, d, valid = slot(j)

        @pl.when(valid)
        def _():
            @pl.when(ky != y)
            def _():
                kv_arrived(j)

            stats_block(0, j, d)

        return carry

    lax.fori_loop(0, SLOTS, stats_step, 0)

    for copy in to_corner:
        copy.wait()
    for b in range(2, 4):
        qt[:, b * 2 * R:(b + 1) * 2 * R] = qc[b * 2 * R:(b + 1) * 2 * R, :].T
        ot[:, b * 2 * R:(b + 1) * 2 * R] = oc[b * 2 * R:(b + 1) * 2 * R, :].T

    def stats_other(j, carry):
        a, ky, d, valid = slot(j)

        @pl.when(valid)
        def _():
            stats_block(1, j, d)

        return carry

    lax.fori_loop(0, SLOTS, stats_other, 0)

    peers = (mate, zmate, corner)
    swaps = [remote(stat, stat_in.at[i], ss_sem.at[i], sr_sem.at[i], peers[i]) for i in range(3)]

    @pl.when(around)
    def _():
        pl.semaphore_wait(in_sem, 1)

    for copy in swaps:
        copy.start()
    for copy in swaps:
        copy.wait()
    for r in range(4):
        def rows_of(kind, r=r):
            mine = [stat[8 * kind + 2 * r:8 * kind + 2 * r + 2, :]]
            for i in range(3):
                there = 8 * kind + 2 * (r ^ (i + 1))
                mine.append(stat_in[i, there:there + 2, :])
            return mine

        tops = rows_of(0)
        top = jnp.maximum(jnp.maximum(tops[0], tops[1]), jnp.maximum(tops[2], tops[3]))
        factors = [jnp.exp2(t - top) for t in tops]
        total = sum(f * t for f, t in zip(factors, rows_of(1)))
        weighted = sum(f * t for f, t in zip(factors, rows_of(2)))
        norm[2 * r:2 * r + 2, :] = top + jnp.log2(total)
        norm[8 + 2 * r:8 + 2 * r + 2, :] = weighted / total

    def part_copy(j):
        a, ky, d, valid = slot(j)
        tx = x - 3 * lax.div(a, 3)
        return remote(part.at[j], got.at[a, y], ps_sem.at[j], pr_sem.at[a, y], at(tx, ky))

    def part_arrived(a, sy):
        remote(got.at[a, sy], got.at[a, sy], ps_sem.at[0], pr_sem.at[a, sy], mate).wait_recv()

    def gather_row(a, e, cond):
        sy = lax.rem(y + e, SIDE)

        @pl.when(cond)
        def _():
            part_arrived(a, sy)
            accf[a] += got[a, sy].astype(jnp.float32)

    def x_hand_over(a):
        for e in range(1, SIDE):
            wraps = y + e >= SIDE
            reaches = True if a == 1 else (wraps | (core == 1) if e == 1 else wraps)
            gather_row(a, e, x_here[a] & reaches)

        @pl.when(x_here[a])
        def _():
            xout[a - 1] = accf[a].astype(jnp.bfloat16)
            x_copy[a].start()

    x_here = {1: (x >= 1) & jnp.logical_not(holds), 2: (x >= 2) & holds}
    x_copy = {
        a: remote(xout.at[a - 1], xin.at[a - 1], xs_sem.at[a - 1], xr_sem.at[a - 1],
                  at(lax.rem(x - a + SIDE, SIDE), y))
        for a in (1, 2)
    }

    def grads_step(i, carry):
        j = SLOTS - 1 - i
        a, ky, d, valid = slot(j)

        @pl.when(j == 1)
        def _():
            x_hand_over(2)

        @pl.when(valid)
        def _():
            plow, slow = [], []
            for g in range(8):
                sl = slice(g * R, (g + 1) * R)
                factor = jnp.exp2(mrun[j, g:g + 1, :] - norm[g:g + 1, :])
                p = prob[j, :, sl] * factor
                plow.append(p.astype(jnp.bfloat16))
                slow.append((p * (dprob[j, :, sl] - norm[8 + g:9 + g, :])).astype(jnp.bfloat16))
            keys = kv[j, :, 0:HD]
            dk = jnp.dot(jnp.concatenate(slow, axis=1), qc[...], preferred_element_type=jnp.float32)
            dv = jnp.dot(jnp.concatenate(plow, axis=1), oc[...], preferred_element_type=jnp.float32)

            @pl.when(ky == y)
            def _():
                accf[a, :, 0:HD] = dk
                accf[a, :, HD:2 * HD] = dv

            @pl.when(ky != y)
            def _():
                part[j, :, 0:HD] = dk.astype(jnp.bfloat16)
                part[j, :, HD:2 * HD] = dv.astype(jnp.bfloat16)
                part_copy(j).start()

            for r in range(4):
                dqt[r] += lax.dot_general(
                    keys, jnp.concatenate(slow[2 * r:2 * r + 2], axis=1),
                    (((0,), (0,)), ((), ())), preferred_element_type=jnp.float32,
                )

        return carry

    lax.fori_loop(0, SLOTS, grads_step, 0)

    dq_swaps = [
        remote(dqt.at[2 * i + 1], dq_in.at[i], ds_sem.at[i], dr_sem.at[i], mate) for i in range(2)
    ]
    for copy in dq_swaps:
        copy.start()

    x_hand_over(1)
    for copy in dq_swaps:
        copy.wait()
    zq_out[...] = (dqt[2] + dq_in[1]).astype(jnp.bfloat16)
    zq_swap = remote(zq_out, zq_in, ds_sem.at[2], dr_sem.at[2], zmate)
    zq_swap.start()

    for e in range(1, SIDE):
        gather_row(0, e, holds & (y + e < SIDE))

    for a in (1, 2):
        @pl.when(holds & (x + a < SIDE))
        def _():
            remote(xin.at[a - 1], xin.at[a - 1], xs_sem.at[0], xr_sem.at[a - 1], mate).wait_recv()
            accf[0] += xin[a - 1].astype(jnp.float32)

    @pl.when(far_out)
    def _():
        part_arrived(3, 0)
        accf[0] += got[3, 0].astype(jnp.float32)

    wide_out = HD // share
    pair = lax.div(member, 2)
    z_sends = []
    for e in range(1, share):
        to = lax.rem(member + e, share)
        z_sends.append(
            remote(zout.at[to], zin.at[pair], zs_sem.at[to], zr_sem.at[pair], (grp - member + to, srv))
        )

    @pl.when(holds)
    def _():
        turned = accf[0].T
        for m in range(share):
            for s in range(2):
                piece = turned[s * HD + m * wide_out:s * HD + (m + 1) * wide_out, :]
                zown[m, s * wide_out:(s + 1) * wide_out, :] = piece
                zout[m, s * wide_out:(s + 1) * wide_out, :] = piece.astype(jnp.bfloat16)
        for copy in z_sends:
            copy.start()
        zsum[...] = zown[member]

    @pl.when(jnp.logical_not(holds))
    def _():
        zsum[...] = jnp.zeros_like(zsum)

    zq_swap.wait()
    mixed = dqt[0] + dq_in[0] + zq_in[...].astype(jnp.float32)
    for h in range(2):
        dq_out[:, h * HD:(h + 1) * HD] = (mixed[:, h * R:(h + 1) * R].T * SCALE).astype(jnp.bfloat16)

    for w in range(share // 2):
        @pl.when(jnp.logical_not(holds & (pair == w)))
        def _():
            remote(zin.at[w], zin.at[w], zs_sem.at[0], zr_sem.at[w], mate).wait_recv()
            zsum[...] += zin[w].astype(jnp.float32)

    dk_out[...] = (zsum[0:wide_out, :] * SCALE).astype(jnp.bfloat16)
    dv_out[...] = zsum[wide_out:2 * wide_out, :].astype(jnp.bfloat16)

    for cond, copy in own_sends + near_sends + next_sends + [(x_here[a], x_copy[a]) for a in (1, 2)]:
        pl.when(cond)(copy.wait_send)

    def parts_sent(j, carry):
        a, ky, d, valid = slot(j)

        @pl.when(valid & (ky != y))
        def _():
            part_copy(j).wait_send()

        return carry

    lax.fori_loop(0, SLOTS, parts_sent, 0)
    for copy in z_sends:
        pl.when(holds)(copy.wait_send)


def write_out(a_ref, b_ref, c_ref, a_out, b_out, c_out, sem):
    copies = [
        pltpu.make_async_copy(src, dst, sem.at[i])
        for i, (src, dst) in enumerate(((a_ref, a_out), (b_ref, b_out), (c_ref, c_out)))
    ]
    for copy in copies:
        copy.start()
    for copy in copies:
        copy.wait()


def on_device(queries, key_rows, value_rows, grad_output, doc_ids):
    R = queries.shape[0]
    share = lax.axis_size("grp") // (key_rows.shape[1] // HD)
    wide = min(128, R)
    docs = doc_ids.reshape(-1, wide)
    bf, f32, i32 = jnp.bfloat16, jnp.float32, jnp.int32
    dma = pltpu.SemaphoreType.DMA
    scratch = [
        pltpu.VMEM(docs.shape, i32),
        pltpu.VMEM((SLOTS, R, 2 * HD), bf),
        pltpu.VMEM((8 * R, HD), bf),
        pltpu.VMEM((8 * R, HD), bf),
        pltpu.VMEM((HD, 8 * R), bf),
        pltpu.VMEM((HD, 8 * R), bf),
        pltpu.VMEM((2, R), i32),
        pltpu.VMEM((2, R), i32),
        pltpu.VMEM((SLOTS, R, 8 * R), f32),
        pltpu.VMEM((SLOTS, R, 8 * R), f32),
        pltpu.VMEM((SLOTS, 8, R), f32),
        pltpu.VMEM((24, R), f32),
        pltpu.VMEM((3, 24, R), f32),
        pltpu.VMEM((16, R), f32),
        pltpu.VMEM((4, HD, 2 * R), f32),
        pltpu.VMEM((2, HD, 2 * R), f32),
        pltpu.VMEM((HD, 2 * R), bf),
        pltpu.VMEM((HD, 2 * R), bf),
        pltpu.VMEM((SLOTS, R, 2 * HD), bf),
        pltpu.VMEM((4, SIDE, R, 2 * HD), bf),
        pltpu.VMEM((3, R, 2 * HD), f32),
        pltpu.VMEM((2, R, 2 * HD), bf),
        pltpu.VMEM((2, R, 2 * HD), bf),
        pltpu.VMEM((share, 2 * HD // share, R), f32),
        pltpu.VMEM((share, 2 * HD // share, R), bf),
        pltpu.VMEM((share // 2, 2 * HD // share, R), bf),
        pltpu.VMEM((2 * HD // share, R), f32),
        dma((7,)), dma((6,)), dma((6,)), dma((12,)), dma((SLOTS,)), dma((3,)), dma((3,)),
        dma((SLOTS,)), dma((4, SIDE)), dma((2,)), dma((2,)), dma((share,)), dma((share // 2,)),
        dma((3,)), dma((3,)), pltpu.SemaphoreType.REGULAR,
    ]
    vmem = pl.BlockSpec(memory_space=pltpu.VMEM)
    hbm = pl.BlockSpec(memory_space=pltpu.HBM)
    dq, dk, dv = pl.pallas_call(
        functools.partial(kernel, share),
        out_shape=(
            pltpu.VMEM((R, 2 * HD), bf),
            pltpu.VMEM((HD // share, R), bf),
            pltpu.VMEM((HD // share, R), bf),
        ),
        in_specs=[hbm, hbm, hbm, hbm, hbm],
        out_specs=(vmem, vmem, vmem),
        scratch_shapes=scratch,
        compiler_params=pltpu.CompilerParams(
            collective_id=0, has_side_effects=True, vmem_limit_bytes=56 * 1024 * 1024
        ),
    )(*(pltpu.with_memory_space_constraint(t, pltpu.HBM) for t in (queries, key_rows, value_rows, grad_output, docs)))
    dq, dk, dv = pl.pallas_call(
        write_out,
        out_shape=tuple(jax.ShapeDtypeStruct(part.shape, part.dtype) for part in (dq, dk, dv)),
        in_specs=[vmem, vmem, vmem],
        out_specs=(hbm, hbm, hbm),
        scratch_shapes=[dma((3,))],
    )(*(pltpu.with_memory_space_constraint(t, pltpu.VMEM) for t in (dq, dk, dv)))
    return dq, dk.T, dv.T


def solution(mesh):
    in_specs = (P("srv", "grp"), P("srv", None), P("srv", None), P("srv", "grp"), P())
    out_specs = (P("srv", "grp"), P("srv", "grp"), P("srv", "grp"))
    return jax.shard_map(
        on_device, mesh=mesh, in_specs=in_specs, out_specs=out_specs, check_vma=False
    )
```

```python
import functools
import math

import jax
import jax.numpy as jnp
from jax import lax
from jax.experimental import pallas as pl
from jax.experimental.pallas import tpu as pltpu
from jax.sharding import PartitionSpec as P

HD = 128
SIDE = 4
SLOTS = 7
HIDDEN = -1e30
MESH = pl.DeviceIdType.MESH
SCALE = HD ** -0.5
SCALE2 = SCALE * math.log2(math.e)


def kernel(
    share, q_ref, k_ref, v_ref, o_ref, doc_hbm,
    dq_out, dk_out, dv_out,
    doc_ref, kv, qc, oc, qt, ot, marks, high, prob, dprob, mrun, gscore, stat, stat_in, norm,
    dqt, dq_in, zq_out, zq_in, part, got, accf, xout, xin, zown, zout, zin, zsum,
    loc_sem, qs_sem, qr_sem, ks_sem, kr_sem, ss_sem, sr_sem, ps_sem, pr_sem,
    xs_sem, xr_sem, zs_sem, zr_sem, ds_sem, dr_sem, in_sem,
):
    R = q_ref.shape[0]
    grp = lax.axis_index("grp")
    srv = lax.axis_index("srv")
    core = lax.rem(srv, 2)
    chip = lax.div(srv, 2)
    y = lax.rem(chip, SIDE)
    x = lax.div(chip, SIDE)
    member = lax.rem(grp, share)
    kv_head = lax.div(grp, share)
    plane = lax.rem(grp, 2)
    mate = (grp, srv + 1 - 2 * core)
    zmate = (grp + 1 - 2 * plane, srv)
    corner = (grp + 1 - 2 * plane, srv + 1 - 2 * core)
    side = lax.rem(x + y, 2)
    holds = side == plane
    column = lax.div(y, 2)

    def at(cx, cy):
        return (grp, (cx * SIDE + cy) * 2 + core)

    def remote(src, dst, ssem, rsem, device):
        return pltpu.make_async_remote_copy(
            src_ref=src, dst_ref=dst, send_sem=ssem, recv_sem=rsem,
            device_id=device, device_id_type=MESH,
        )

    col = pl.ds(pl.multiple_of(kv_head * HD, HD), HD)
    local_kv = [
        pltpu.make_async_copy(k_ref.at[:, col], kv.at[column, :, pl.ds(0, HD)], loc_sem.at[0]),
        pltpu.make_async_copy(v_ref.at[:, col], kv.at[column, :, pl.ds(HD, HD)], loc_sem.at[1]),
    ]
    local_q = []
    for h in range(2):
        rows = pl.ds(h * R, R)
        cols = pl.ds(h * HD, HD)
        local_q.append(pltpu.make_async_copy(q_ref.at[:, cols], qc.at[rows], loc_sem.at[2 + 2 * h]))
        local_q.append(pltpu.make_async_copy(o_ref.at[:, cols], oc.at[rows], loc_sem.at[3 + 2 * h]))
    local_doc = pltpu.make_async_copy(doc_hbm, doc_ref, loc_sem.at[6])
    local_doc.start()
    for copy in local_kv:
        pl.when(holds)(copy.start)
    for copy in local_q:
        copy.start()

    barrier = pltpu.get_barrier_semaphore()

    def greet(device):
        pl.semaphore_signal(barrier, inc=1, device_id=device, device_id_type=MESH)

    far_out = (chip == 3) & (core == 1) & (plane == 1)
    far_in = (chip == 12) & (core == 1) & (plane == 1)
    everyone = [mate, corner]
    for e in range(1, SIDE):
        everyone += [at(x, lax.rem(y + e, SIDE)), at(lax.rem(x + e, SIDE), y)]
    for e in range(1, share):
        everyone.append((grp - member + lax.rem(member + e, share), srv))

    leader = (member == 0) & (srv == 0)
    beside = ((member == 0) & (srv == 1)) | ((member == 1) & (srv == 0))
    around = (
        ((member == 0) & (core == 0) & (chip > 0) & ((x == 0) | (y == 0)))
        | ((member == 1) & (srv == 1)) | ((member >= 2) & (srv == 0))
    )

    @pl.when(jnp.logical_not(leader))
    def _():
        for device in everyone:
            greet(device)

    @pl.when(far_out)
    def _():
        greet(at(3, 0))

    @pl.when(far_in)
    def _():
        greet(at(0, 3))

    local_doc.wait()
    wide = doc_ref.shape[1]
    per = R // wide
    number = lax.broadcasted_iota(jnp.int32, (32, wide), 0)
    lane = lax.broadcasted_iota(jnp.int32, (1, wide), 1)
    qt[HD + 32:2 * HD, :] = jnp.zeros((HD - 32, 8 * R), jnp.bfloat16)
    for b in range(2):
        block = chip * 2 + (core if b == 0 else 1 - core)
        for t in range(per):
            row = block * per + t
            own = doc_ref[pl.ds(row, 1), :]
            fence = jnp.where(own == number, 0.0, HIDDEN).astype(jnp.bfloat16)
            high[b:b + 1, t * wide:(t + 1) * wide] = lane + row * wide
            for g in (2 * b, 2 * b + 1, 2 * b + 4, 2 * b + 5):
                qt[HD:HD + 32, g * R + t * wide:g * R + (t + 1) * wide] = fence

    stat[0:8, :] = jnp.full((8, R), HIDDEN, jnp.float32)
    stat[8:24, :] = jnp.zeros((16, R), jnp.float32)
    dqt[...] = jnp.zeros_like(dqt)

    far = jnp.where(far_out | far_in, 1, 0)
    pl.semaphore_wait(barrier, 2 + 2 * (SIDE - 1) + share - 1 + far - jnp.where(beside | around, 1, 0))

    @pl.when(leader)
    def _():
        for device in everyone:
            pl.semaphore_signal(in_sem, inc=1, device_id=device, device_id_type=MESH)

    def swap(n, src, dst, device):
        return [
            remote(ref.at[pl.ds(src * 2 * R, 2 * R)], ref.at[pl.ds(dst * 2 * R, 2 * R)],
                   qs_sem.at[2 * n + i], qr_sem.at[2 * n + i], device)
            for i, ref in enumerate((qc, oc))
        ]

    to_core, to_plane, to_corner = swap(0, 0, 1, mate), swap(1, 0, 2, zmate), swap(2, 2, 3, mate)

    def kv_send(n, src, dst, device):
        return [
            remote(kv.at[src, pl.ds(i * half, half)], kv.at[dst, pl.ds(i * half, half)],
                   ks_sem.at[n, i], kr_sem.at[dst, i], device)
            for i in range(2)
        ]

    half = R // 2
    own_sends, near_sends, next_sends = [], [], []
    for e in range(1, 3):
        own_sends.append(
            (holds & (x + e < SIDE), kv_send(e - 1, column, 2 * e + column, at(lax.rem(x + e, SIDE), y)))
        )
    own_sends.append((far_out, kv_send(2, column, 6, at(3, 0))))
    for e in range(1, SIDE):
        there = at(x, lax.rem(y + e, SIDE))
        wraps = y + e >= SIDE
        own_sends.append((holds & jnp.logical_not(wraps), kv_send(2 + e, column, column, there)))
        near_sends.append(
            (jnp.logical_not(holds) & (x >= 1), kv_send(5 + e, 2 + column, 2 + column, there))
        )
        reaches = wraps | (core == 1) if e == 1 else wraps
        next_sends.append((holds & (x >= 2) & reaches, kv_send(8 + e, 4 + column, 4 + column, there)))

    def start_all(sends, i):
        for cond, copies in sends:
            pl.when(cond)(copies[i].start)

    for copy in local_kv:
        pl.when(holds)(copy.wait)
    for i in range(2):
        start_all(own_sends, i)
    for copy in local_q:
        copy.wait()

    @pl.when(beside)
    def _():
        pl.semaphore_wait(in_sem, 1)

    for copy in to_plane + to_core:
        copy.start()
    for copy in to_core:
        copy.wait()
    for b in range(2):
        qt[0:HD, b * 2 * R:(b + 1) * 2 * R] = qc[b * 2 * R:(b + 1) * 2 * R, :].T
        ot[:, b * 2 * R:(b + 1) * 2 * R] = oc[b * 2 * R:(b + 1) * 2 * R, :].T

    def kv_half(j, i):
        rows = kv.at[j, pl.ds(i * half, half)]
        remote(rows, rows, ks_sem.at[0, 0], kr_sem.at[j, i], mate).wait_recv()

    def kv_arrived(j):
        for i in range(2):
            kv_half(j, i)

    def slot(j):
        a = lax.div(j, 2)
        ky = jnp.where(a == 3, SIDE - 1, lax.rem(plane + x + a, 2) + 2 * lax.rem(j, 2))
        d = 4 * a + y - ky
        valid = (x >= a) & (d >= 0) & (d <= 8 + core) & ((a < 3) | (plane == 1))
        return a, ky, d, valid

    row_in_block = lax.broadcasted_iota(jnp.int32, (R, R), 0)

    def mark_documents(j, d):
        for t in range(per):
            own = doc_ref[pl.ds(((chip - d) * 2 + core) * per + t, 1), :]
            hot = jnp.where(own == number, 1.0, 0.0)
            hot = jnp.concatenate([hot, jnp.zeros((HD - 32, wide), jnp.float32)], axis=0)
            marks[j, t * wide:(t + 1) * wide, :] = hot.T.astype(jnp.bfloat16)

    def stats_block(z, j, d):
        @pl.when(d == 0)
        def _():
            stats_groups(z, j, True)

        @pl.when(d != 0)
        def _():
            stats_groups(z, j, False)

    def stats_groups(z, j, diagonal):
        key_pos = row_in_block + (chip * 2 + core) * R
        keys = jnp.concatenate([kv[j, :, 0:HD], marks[j]], axis=1)
        values = kv[j, :, HD:2 * HD]
        for g in range(4 * z, 4 * z + 4):
            b = (g // 2) % 2
            sl = slice(g * R, (g + 1) * R)
            s = jnp.dot(keys, qt[:, sl], preferred_element_type=jnp.float32) * SCALE2
            if diagonal:
                s = jnp.where(key_pos <= high[b:b + 1, :], s, HIDDEN)
            m_old = stat[g:g + 1, :]
            m_new = jnp.maximum(m_old, jnp.max(s, axis=0, keepdims=True))
            alpha = jnp.exp2(m_old - m_new)
            p = jnp.exp2(s - m_new)
            dp = jnp.dot(values, ot[:, sl], preferred_element_type=jnp.float32)
            stat[g:g + 1, :] = m_new
            stat[8 + g:9 + g, :] = stat[8 + g:9 + g, :] * alpha + jnp.sum(p, axis=0, keepdims=True)
            stat[16 + g:17 + g, :] = stat[16 + g:17 + g, :] * alpha + jnp.sum(p * dp, axis=0, keepdims=True)
            mrun[j, g:g + 1, :] = m_new
            prob[j, :, sl] = p
            dprob[j, :, sl] = dp

    def stats_step(j, carry):
        @pl.when((j == 1) & (x >= 1) & jnp.logical_not(holds))
        def _():
            for i in range(2):
                kv_half(2 + column, i)
                start_all(near_sends, i)

        @pl.when((j == 2) & (x >= 2) & holds)
        def _():
            for i in range(2):
                kv_half(4 + column, i)
                start_all(next_sends, i)

        @pl.when(j == 4)
        def _():
            for copy in to_plane:
                copy.wait()
            for copy in to_corner:
                copy.start()

        a, ky, d, valid = slot(j)

        @pl.when(valid)
        def _():
            @pl.when(ky != y)
            def _():
                kv_arrived(j)

            mark_documents(j, d)
            stats_block(0, j, d)

        return carry

    lax.fori_loop(0, SLOTS, stats_step, 0)

    for copy in to_corner:
        copy.wait()
    for b in range(2, 4):
        qt[0:HD, b * 2 * R:(b + 1) * 2 * R] = qc[b * 2 * R:(b + 1) * 2 * R, :].T
        ot[:, b * 2 * R:(b + 1) * 2 * R] = oc[b * 2 * R:(b + 1) * 2 * R, :].T

    def stats_other(j, carry):
        a, ky, d, valid = slot(j)

        @pl.when(valid)
        def _():
            stats_block(1, j, d)

        return carry

    lax.fori_loop(0, SLOTS, stats_other, 0)

    peers = (mate, zmate, corner)
    swaps = [remote(stat, stat_in.at[i], ss_sem.at[i], sr_sem.at[i], peers[i]) for i in range(3)]

    @pl.when(around)
    def _():
        pl.semaphore_wait(in_sem, 1)

    for copy in swaps:
        copy.start()
    for copy in swaps:
        copy.wait()
    for r in range(4):
        def rows_of(kind, r=r):
            mine = [stat[8 * kind + 2 * r:8 * kind + 2 * r + 2, :]]
            for i in range(3):
                there = 8 * kind + 2 * (r ^ (i + 1))
                mine.append(stat_in[i, there:there + 2, :])
            return mine

        tops = rows_of(0)
        top = jnp.maximum(jnp.maximum(tops[0], tops[1]), jnp.maximum(tops[2], tops[3]))
        factors = [jnp.exp2(t - top) for t in tops]
        total = sum(f * t for f, t in zip(factors, rows_of(1)))
        weighted = sum(f * t for f, t in zip(factors, rows_of(2)))
        norm[2 * r:2 * r + 2, :] = top + jnp.log2(total)
        norm[8 + 2 * r:8 + 2 * r + 2, :] = weighted / total

    def part_copy(j):
        a, ky, d, valid = slot(j)
        tx = x - 3 * lax.div(a, 3)
        return remote(part.at[j], got.at[a, y], ps_sem.at[j], pr_sem.at[a, y], at(tx, ky))

    def part_arrived(a, sy):
        remote(got.at[a, sy], got.at[a, sy], ps_sem.at[0], pr_sem.at[a, sy], mate).wait_recv()

    def gather_row(a, e, cond):
        sy = lax.rem(y + e, SIDE)

        @pl.when(cond)
        def _():
            part_arrived(a, sy)
            accf[a] += got[a, sy].astype(jnp.float32)

    def x_hand_over(a):
        for e in range(1, SIDE):
            wraps = y + e >= SIDE
            reaches = True if a == 1 else (wraps | (core == 1) if e == 1 else wraps)
            gather_row(a, e, x_here[a] & reaches)

        @pl.when(x_here[a])
        def _():
            xout[a - 1] = accf[a].astype(jnp.bfloat16)
            x_copy[a].start()

    x_here = {1: (x >= 1) & jnp.logical_not(holds), 2: (x >= 2) & holds}
    x_copy = {
        a: remote(xout.at[a - 1], xin.at[a - 1], xs_sem.at[a - 1], xr_sem.at[a - 1],
                  at(lax.rem(x - a + SIDE, SIDE), y))
        for a in (1, 2)
    }

    def grads_step(i, carry):
        j = SLOTS - 1 - i
        a, ky, d, valid = slot(j)

        @pl.when(j == 1)
        def _():
            x_hand_over(2)

        @pl.when(valid)
        def _():
            plow, slow = [], []
            for g in range(8):
                sl = slice(g * R, (g + 1) * R)
                factor = jnp.exp2(mrun[j, g:g + 1, :] - norm[g:g + 1, :])
                p = prob[j, :, sl] * factor
                plow.append(p.astype(jnp.bfloat16))
                slow.append((p * (dprob[j, :, sl] - norm[8 + g:9 + g, :])).astype(jnp.bfloat16))
            dk = jnp.dot(jnp.concatenate(slow, axis=1), qc[...], preferred_element_type=jnp.float32)
            dv = jnp.dot(jnp.concatenate(plow, axis=1), oc[...], preferred_element_type=jnp.float32)

            @pl.when(ky == y)
            def _():
                accf[a, :, 0:HD] = dk
                accf[a, :, HD:2 * HD] = dv

            @pl.when(ky != y)
            def _():
                part[j, :, 0:HD] = dk.astype(jnp.bfloat16)
                part[j, :, HD:2 * HD] = dv.astype(jnp.bfloat16)
                part_copy(j).start()

            for g in range(8):
                gscore[j, :, g * R:(g + 1) * R] = slow[g]

        return carry

    lax.fori_loop(0, SLOTS, grads_step, 0)

    def query_step(j, carry):
        a, ky, d, valid = slot(j)

        @pl.when(valid)
        def _():
            keys = kv[j, :, 0:HD]
            for r in range(4):
                dqt[r] += lax.dot_general(
                    keys, gscore[j, :, r * 2 * R:(r + 1) * 2 * R],
                    (((0,), (0,)), ((), ())), preferred_element_type=jnp.float32,
                )

        return carry

    lax.fori_loop(0, SLOTS, query_step, 0)

    dq_swaps = [
        remote(dqt.at[2 * i + 1], dq_in.at[i], ds_sem.at[i], dr_sem.at[i], mate) for i in range(2)
    ]
    for copy in dq_swaps:
        copy.start()

    x_hand_over(1)
    for copy in dq_swaps:
        copy.wait()
    zq_out[...] = (dqt[2] + dq_in[1]).astype(jnp.bfloat16)
    zq_swap = remote(zq_out, zq_in, ds_sem.at[2], dr_sem.at[2], zmate)
    zq_swap.start()

    for e in range(1, SIDE):
        gather_row(0, e, holds & (y + e < SIDE))

    for a in (1, 2):
        @pl.when(holds & (x + a < SIDE))
        def _():
            remote(xin.at[a - 1], xin.at[a - 1], xs_sem.at[0], xr_sem.at[a - 1], mate).wait_recv()
            accf[0] += xin[a - 1].astype(jnp.float32)

    @pl.when(far_out)
    def _():
        part_arrived(3, 0)
        accf[0] += got[3, 0].astype(jnp.float32)

    wide_out = HD // share
    pair = lax.div(member, 2)
    z_sends = []
    for e in range(1, share):
        to = lax.rem(member + e, share)
        z_sends.append(
            remote(zout.at[to], zin.at[pair], zs_sem.at[to], zr_sem.at[pair], (grp - member + to, srv))
        )

    @pl.when(holds)
    def _():
        turned = accf[0].T
        for m in range(share):
            for s in range(2):
                piece = turned[s * HD + m * wide_out:s * HD + (m + 1) * wide_out, :]
                zown[m, s * wide_out:(s + 1) * wide_out, :] = piece
                zout[m, s * wide_out:(s + 1) * wide_out, :] = piece.astype(jnp.bfloat16)
        for copy in z_sends:
            copy.start()
        zsum[...] = zown[member]

    @pl.when(jnp.logical_not(holds))
    def _():
        zsum[...] = jnp.zeros_like(zsum)

    zq_swap.wait()
    mixed = dqt[0] + dq_in[0] + zq_in[...].astype(jnp.float32)
    for h in range(2):
        dq_out[:, h * HD:(h + 1) * HD] = (mixed[:, h * R:(h + 1) * R].T * SCALE).astype(jnp.bfloat16)

    for w in range(share // 2):
        @pl.when(jnp.logical_not(holds & (pair == w)))
        def _():
            remote(zin.at[w], zin.at[w], zs_sem.at[0], zr_sem.at[w], mate).wait_recv()
            zsum[...] += zin[w].astype(jnp.float32)

    dk_out[...] = (zsum[0:wide_out, :] * SCALE).astype(jnp.bfloat16)
    dv_out[...] = zsum[wide_out:2 * wide_out, :].astype(jnp.bfloat16)

    for cond, copies in own_sends + near_sends + next_sends + [(x_here[a], [x_copy[a]]) for a in (1, 2)]:
        for copy in copies:
            pl.when(cond)(copy.wait_send)

    def parts_sent(j, carry):
        a, ky, d, valid = slot(j)

        @pl.when(valid & (ky != y))
        def _():
            part_copy(j).wait_send()

        return carry

    lax.fori_loop(0, SLOTS, parts_sent, 0)
    for copy in z_sends:
        pl.when(holds)(copy.wait_send)


def write_out(a_ref, b_ref, c_ref, a_out, b_out, c_out, sem):
    copies = [
        pltpu.make_async_copy(src, dst, sem.at[i])
        for i, (src, dst) in enumerate(((a_ref, a_out), (b_ref, b_out), (c_ref, c_out)))
    ]
    for copy in copies:
        copy.start()
    for copy in copies:
        copy.wait()


def on_device(queries, key_rows, value_rows, grad_output, doc_ids):
    R = queries.shape[0]
    share = lax.axis_size("grp") // (key_rows.shape[1] // HD)
    wide = min(128, R)
    docs = doc_ids.reshape(-1, wide)
    bf, f32, i32 = jnp.bfloat16, jnp.float32, jnp.int32
    dma = pltpu.SemaphoreType.DMA
    scratch = [
        pltpu.VMEM(docs.shape, i32),
        pltpu.VMEM((SLOTS, R, 2 * HD), bf),
        pltpu.VMEM((8 * R, HD), bf),
        pltpu.VMEM((8 * R, HD), bf),
        pltpu.VMEM((2 * HD, 8 * R), bf),
        pltpu.VMEM((HD, 8 * R), bf),
        pltpu.VMEM((SLOTS, R, HD), bf),
        pltpu.VMEM((2, R), i32),
        pltpu.VMEM((SLOTS, R, 8 * R), f32),
        pltpu.VMEM((SLOTS, R, 8 * R), f32),
        pltpu.VMEM((SLOTS, 8, R), f32),
        pltpu.VMEM((SLOTS, R, 8 * R), bf),
        pltpu.VMEM((24, R), f32),
        pltpu.VMEM((3, 24, R), f32),
        pltpu.VMEM((16, R), f32),
        pltpu.VMEM((4, HD, 2 * R), f32),
        pltpu.VMEM((2, HD, 2 * R), f32),
        pltpu.VMEM((HD, 2 * R), bf),
        pltpu.VMEM((HD, 2 * R), bf),
        pltpu.VMEM((SLOTS, R, 2 * HD), bf),
        pltpu.VMEM((4, SIDE, R, 2 * HD), bf),
        pltpu.VMEM((3, R, 2 * HD), f32),
        pltpu.VMEM((2, R, 2 * HD), bf),
        pltpu.VMEM((2, R, 2 * HD), bf),
        pltpu.VMEM((share, 2 * HD // share, R), f32),
        pltpu.VMEM((share, 2 * HD // share, R), bf),
        pltpu.VMEM((share // 2, 2 * HD // share, R), bf),
        pltpu.VMEM((2 * HD // share, R), f32),
        dma((7,)), dma((6,)), dma((6,)), dma((12, 2)), dma((SLOTS, 2)), dma((3,)), dma((3,)),
        dma((SLOTS,)), dma((4, SIDE)), dma((2,)), dma((2,)), dma((share,)), dma((share // 2,)),
        dma((3,)), dma((3,)), pltpu.SemaphoreType.REGULAR,
    ]
    vmem = pl.BlockSpec(memory_space=pltpu.VMEM)
    hbm = pl.BlockSpec(memory_space=pltpu.HBM)
    dq, dk, dv = pl.pallas_call(
        functools.partial(kernel, share),
        out_shape=(
            pltpu.VMEM((R, 2 * HD), bf),
            pltpu.VMEM((HD // share, R), bf),
            pltpu.VMEM((HD // share, R), bf),
        ),
        in_specs=[hbm, hbm, hbm, hbm, hbm],
        out_specs=(vmem, vmem, vmem),
        scratch_shapes=scratch,
        compiler_params=pltpu.CompilerParams(
            collective_id=0, has_side_effects=True, vmem_limit_bytes=56 * 1024 * 1024
        ),
    )(*(pltpu.with_memory_space_constraint(t, pltpu.HBM) for t in (queries, key_rows, value_rows, grad_output, docs)))
    dq, dk, dv = pl.pallas_call(
        write_out,
        out_shape=tuple(jax.ShapeDtypeStruct(part.shape, part.dtype) for part in (dq, dk, dv)),
        in_specs=[vmem, vmem, vmem],
        out_specs=(hbm, hbm, hbm),
        scratch_shapes=[dma((3,))],
    )(*(pltpu.with_memory_space_constraint(t, pltpu.VMEM) for t in (dq, dk, dv)))
    return dq, dk.T, dv.T


def solution(mesh):
    in_specs = (P("srv", "grp"), P("srv", None), P("srv", None), P("srv", "grp"), P())
    out_specs = (P("srv", "grp"), P("srv", "grp"), P("srv", "grp"))
    return jax.shard_map(
        on_device, mesh=mesh, in_specs=in_specs, out_specs=out_specs, check_vma=False
    )
```

```python
import functools
import math

import jax
import jax.numpy as jnp
from jax import lax
from jax.experimental import pallas as pl
from jax.experimental.pallas import tpu as pltpu
from jax.sharding import PartitionSpec as P

HD = 128
SIDE = 4
SLOTS = 7
HIDDEN = -1e30
MESH = pl.DeviceIdType.MESH
SCALE = HD ** -0.5
SCALE2 = SCALE * math.log2(math.e)


def kernel(
    share, q_ref, k_ref, v_ref, o_ref, doc_hbm,
    dq_out, dk_out, dv_out,
    doc_ref, kv, qc, oc, qt, ot, marks, high, prob, dprob, mrun, gscore, stat, stat_in, norm,
    dqt, dq_in, zq_out, zq_in, part, got, accf, xout, xin, zown, zout, zin, zsum,
    loc_sem, qs_sem, qr_sem, ks_sem, kr_sem, ss_sem, sr_sem, ps_sem, pr_sem,
    xs_sem, xr_sem, zs_sem, zr_sem, ds_sem, dr_sem, in_sem,
):
    R = q_ref.shape[0]
    grp = lax.axis_index("grp")
    srv = lax.axis_index("srv")
    core = lax.rem(srv, 2)
    chip = lax.div(srv, 2)
    y = lax.rem(chip, SIDE)
    x = lax.div(chip, SIDE)
    member = lax.rem(grp, share)
    kv_head = lax.div(grp, share)
    plane = lax.rem(grp, 2)
    mate = (grp, srv + 1 - 2 * core)
    zmate = (grp + 1 - 2 * plane, srv)
    corner = (grp + 1 - 2 * plane, srv + 1 - 2 * core)
    side = lax.rem(x + y, 2)
    holds = side == plane
    column = lax.div(y, 2)

    def at(cx, cy):
        return (grp, (cx * SIDE + cy) * 2 + core)

    def remote(src, dst, ssem, rsem, device):
        return pltpu.make_async_remote_copy(
            src_ref=src, dst_ref=dst, send_sem=ssem, recv_sem=rsem,
            device_id=device, device_id_type=MESH,
        )

    col = pl.ds(pl.multiple_of(kv_head * HD, HD), HD)
    local_kv = [
        pltpu.make_async_copy(k_ref.at[:, col], kv.at[column, :, pl.ds(0, HD)], loc_sem.at[0]),
        pltpu.make_async_copy(v_ref.at[:, col], kv.at[column, :, pl.ds(HD, HD)], loc_sem.at[1]),
    ]
    local_q = []
    for h in range(2):
        rows = pl.ds(h * R, R)
        cols = pl.ds(h * HD, HD)
        local_q.append(pltpu.make_async_copy(q_ref.at[:, cols], qc.at[rows], loc_sem.at[2 + 2 * h]))
        local_q.append(pltpu.make_async_copy(o_ref.at[:, cols], oc.at[rows], loc_sem.at[3 + 2 * h]))
    local_doc = pltpu.make_async_copy(doc_hbm, doc_ref, loc_sem.at[6])
    local_doc.start()
    for copy in local_kv:
        pl.when(holds)(copy.start)
    for copy in local_q:
        copy.start()

    barrier = pltpu.get_barrier_semaphore()

    def greet(device):
        pl.semaphore_signal(barrier, inc=1, device_id=device, device_id_type=MESH)

    far_out = (chip == 3) & (core == 1) & (plane == 1)
    far_in = (chip == 12) & (core == 1) & (plane == 1)
    everyone = [mate, corner]
    for e in range(1, SIDE):
        everyone += [at(x, lax.rem(y + e, SIDE)), at(lax.rem(x + e, SIDE), y)]
    for e in range(1, share):
        everyone.append((grp - member + lax.rem(member + e, share), srv))

    leader = (member == 0) & (srv == 0)
    beside = ((member == 0) & (srv == 1)) | ((member == 1) & (srv == 0))
    around = (
        ((member == 0) & (core == 0) & (chip > 0) & ((x == 0) | (y == 0)))
        | ((member == 1) & (srv == 1)) | ((member >= 2) & (srv == 0))
    )

    @pl.when(jnp.logical_not(leader))
    def _():
        for device in everyone:
            greet(device)

    @pl.when(far_out)
    def _():
        greet(at(3, 0))

    @pl.when(far_in)
    def _():
        greet(at(0, 3))

    local_doc.wait()
    wide = doc_ref.shape[1]
    per = R // wide
    number = lax.broadcasted_iota(jnp.int32, (32, wide), 0)
    lane = lax.broadcasted_iota(jnp.int32, (1, wide), 1)
    qt[HD + 32:2 * HD, :] = jnp.zeros((HD - 32, 8 * R), jnp.bfloat16)
    for b in range(2):
        block = chip * 2 + (core if b == 0 else 1 - core)
        for t in range(per):
            row = block * per + t
            own = doc_ref[pl.ds(row, 1), :]
            fence = jnp.where(own == number, 0.0, HIDDEN).astype(jnp.bfloat16)
            high[b:b + 1, t * wide:(t + 1) * wide] = lane + row * wide
            for g in (2 * b, 2 * b + 1, 2 * b + 4, 2 * b + 5):
                qt[HD:HD + 32, g * R + t * wide:g * R + (t + 1) * wide] = fence

    stat[0:8, :] = jnp.full((8, R), HIDDEN, jnp.float32)
    stat[8:24, :] = jnp.zeros((16, R), jnp.float32)
    dqt[...] = jnp.zeros_like(dqt)

    far = jnp.where(far_out | far_in, 1, 0)
    pl.semaphore_wait(barrier, 2 + 2 * (SIDE - 1) + share - 1 + far - jnp.where(beside | around, 1, 0))

    @pl.when(leader)
    def _():
        for device in everyone:
            pl.semaphore_signal(in_sem, inc=1, device_id=device, device_id_type=MESH)

    def swap(n, src, dst, device):
        return [
            remote(ref.at[pl.ds(src * 2 * R, 2 * R)], ref.at[pl.ds(dst * 2 * R, 2 * R)],
                   qs_sem.at[2 * n + i], qr_sem.at[2 * n + i], device)
            for i, ref in enumerate((qc, oc))
        ]

    to_core, to_plane, to_corner = swap(0, 0, 1, mate), swap(1, 0, 2, zmate), swap(2, 2, 3, mate)

    def kv_send(n, src, dst, device):
        return [
            remote(kv.at[src, pl.ds(i * half, half)], kv.at[dst, pl.ds(i * half, half)],
                   ks_sem.at[n, i], kr_sem.at[dst, i], device)
            for i in range(2)
        ]

    half = R // 2
    own_sends, near_sends, next_sends = [], [], []
    for e in range(1, 3):
        own_sends.append(
            (holds & (x + e < SIDE), kv_send(e - 1, column, 2 * e + column, at(lax.rem(x + e, SIDE), y)))
        )
    own_sends.append((far_out, kv_send(2, column, 6, at(3, 0))))
    for e in range(1, SIDE):
        there = at(x, lax.rem(y + e, SIDE))
        wraps = y + e >= SIDE
        own_sends.append((holds & jnp.logical_not(wraps), kv_send(2 + e, column, column, there)))
        near_sends.append(
            (jnp.logical_not(holds) & (x >= 1), kv_send(5 + e, 2 + column, 2 + column, there))
        )
        reaches = wraps | (core == 1) if e == 1 else wraps
        next_sends.append((holds & (x >= 2) & reaches, kv_send(8 + e, 4 + column, 4 + column, there)))

    def start_all(sends, i):
        for cond, copies in sends:
            pl.when(cond)(copies[i].start)

    for copy in local_kv:
        pl.when(holds)(copy.wait)
    for i in range(2):
        start_all(own_sends, i)
    for copy in local_q:
        copy.wait()

    @pl.when(beside)
    def _():
        pl.semaphore_wait(in_sem, 1)

    for copy in to_plane + to_core:
        copy.start()
    for copy in to_core:
        copy.wait()
    for b in range(2):
        qt[0:HD, b * 2 * R:(b + 1) * 2 * R] = qc[b * 2 * R:(b + 1) * 2 * R, :].T
        ot[:, b * 2 * R:(b + 1) * 2 * R] = oc[b * 2 * R:(b + 1) * 2 * R, :].T

    def kv_half(j, i):
        rows = kv.at[j, pl.ds(i * half, half)]
        remote(rows, rows, ks_sem.at[0, 0], kr_sem.at[j, i], mate).wait_recv()

    def kv_arrived(j):
        for i in range(2):
            kv_half(j, i)

    def slot(j):
        a = lax.div(j, 2)
        ky = jnp.where(a == 3, SIDE - 1, lax.rem(plane + x + a, 2) + 2 * lax.rem(j, 2))
        d = 4 * a + y - ky
        valid = (x >= a) & (d >= 0) & (d <= 8 + core) & ((a < 3) | (plane == 1))
        return a, ky, d, valid

    row_in_block = lax.broadcasted_iota(jnp.int32, (R, R), 0)

    def mark_documents(j, d):
        for t in range(per):
            own = doc_ref[pl.ds(((chip - d) * 2 + core) * per + t, 1), :]
            hot = jnp.where(own == number, 1.0, 0.0)
            hot = jnp.concatenate([hot, jnp.zeros((HD - 32, wide), jnp.float32)], axis=0)
            marks[j, t * wide:(t + 1) * wide, :] = hot.T.astype(jnp.bfloat16)

    def stats_block(z, j, d):
        @pl.when(d == 0)
        def _():
            stats_groups(z, j, True)

        @pl.when(d != 0)
        def _():
            stats_groups(z, j, False)

    def stats_groups(z, j, diagonal):
        key_pos = row_in_block + (chip * 2 + core) * R
        keys = jnp.concatenate([kv[j, :, 0:HD], marks[j]], axis=1)
        values = kv[j, :, HD:2 * HD]
        for g in range(4 * z, 4 * z + 4):
            b = (g // 2) % 2
            sl = slice(g * R, (g + 1) * R)
            s = jnp.dot(keys, qt[:, sl], preferred_element_type=jnp.float32) * SCALE2
            if diagonal:
                s = jnp.where(key_pos <= high[b:b + 1, :], s, HIDDEN)
            m_old = stat[g:g + 1, :]
            m_new = jnp.maximum(m_old, jnp.max(s, axis=0, keepdims=True))
            alpha = jnp.exp2(m_old - m_new)
            p = jnp.exp2(s - m_new)
            dp = jnp.dot(values, ot[:, sl], preferred_element_type=jnp.float32)
            stat[g:g + 1, :] = m_new
            stat[8 + g:9 + g, :] = stat[8 + g:9 + g, :] * alpha + jnp.sum(p, axis=0, keepdims=True)
            stat[16 + g:17 + g, :] = stat[16 + g:17 + g, :] * alpha + jnp.sum(p * dp, axis=0, keepdims=True)
            mrun[j, g:g + 1, :] = m_new
            prob[j, :, sl] = p
            dprob[j, :, sl] = dp

    def stats_step(j, carry):
        @pl.when((j == 1) & (x >= 1) & jnp.logical_not(holds))
        def _():
            for i in range(2):
                kv_half(2 + column, i)
                start_all(near_sends, i)

        @pl.when((j == 2) & (x >= 2) & holds)
        def _():
            for i in range(2):
                kv_half(4 + column, i)
                start_all(next_sends, i)

        @pl.when(j == 4)
        def _():
            for copy in to_plane:
                copy.wait()
            for copy in to_corner:
                copy.start()

        a, ky, d, valid = slot(j)

        @pl.when(valid)
        def _():
            @pl.when(ky != y)
            def _():
                kv_arrived(j)

            mark_documents(j, d)
            stats_block(0, j, d)

        return carry

    lax.fori_loop(0, SLOTS, stats_step, 0)

    for copy in to_corner:
        copy.wait()
    for b in range(2, 4):
        qt[0:HD, b * 2 * R:(b + 1) * 2 * R] = qc[b * 2 * R:(b + 1) * 2 * R, :].T
        ot[:, b * 2 * R:(b + 1) * 2 * R] = oc[b * 2 * R:(b + 1) * 2 * R, :].T

    def stats_other(j, carry):
        a, ky, d, valid = slot(j)

        @pl.when(valid)
        def _():
            stats_block(1, j, d)

        return carry

    lax.fori_loop(0, SLOTS, stats_other, 0)

    peers = (mate, zmate, corner)
    swaps = [remote(stat, stat_in.at[i], ss_sem.at[i], sr_sem.at[i], peers[i]) for i in range(3)]

    @pl.when(around)
    def _():
        pl.semaphore_wait(in_sem, 1)

    for copy in swaps:
        copy.start()
    for copy in swaps:
        copy.wait()
    for r in range(4):
        def rows_of(kind, r=r):
            mine = [stat[8 * kind + 2 * r:8 * kind + 2 * r + 2, :]]
            for i in range(3):
                there = 8 * kind + 2 * (r ^ (i + 1))
                mine.append(stat_in[i, there:there + 2, :])
            return mine

        tops = rows_of(0)
        top = jnp.maximum(jnp.maximum(tops[0], tops[1]), jnp.maximum(tops[2], tops[3]))
        factors = [jnp.exp2(t - top) for t in tops]
        total = sum(f * t for f, t in zip(factors, rows_of(1)))
        weighted = sum(f * t for f, t in zip(factors, rows_of(2)))
        norm[2 * r:2 * r + 2, :] = top + jnp.log2(total)
        norm[8 + 2 * r:8 + 2 * r + 2, :] = weighted / total

    def part_copy(j):
        a, ky, d, valid = slot(j)
        tx = x - 3 * lax.div(a, 3)
        return [
            remote(part.at[j, pl.ds(i * half, half)], got.at[a, y, pl.ds(i * half, half)],
                   ps_sem.at[j, i], pr_sem.at[a, y, i], at(tx, ky))
            for i in range(2)
        ]

    def part_arrived(a, sy, i):
        rows = got.at[a, sy, pl.ds(i * half, half)]
        remote(rows, rows, ps_sem.at[0, 0], pr_sem.at[a, sy, i], mate).wait_recv()

    def gather_row(a, e, i, cond):
        sy = lax.rem(y + e, SIDE)
        rows = slice(i * half, (i + 1) * half)

        @pl.when(cond)
        def _():
            part_arrived(a, sy, i)
            accf[a, rows, :] += got[a, sy, rows, :].astype(jnp.float32)

    def x_hand_over(a):
        for i in range(2):
            rows = slice(i * half, (i + 1) * half)
            for e in range(1, SIDE):
                wraps = y + e >= SIDE
                reaches = True if a == 1 else (wraps | (core == 1) if e == 1 else wraps)
                gather_row(a, e, i, x_here[a] & reaches)

            @pl.when(x_here[a])
            def _(i=i, rows=rows):
                xout[a - 1, rows, :] = accf[a, rows, :].astype(jnp.bfloat16)
                x_copy[a][i].start()

    x_here = {1: (x >= 1) & jnp.logical_not(holds), 2: (x >= 2) & holds}
    x_copy = {
        a: [
            remote(xout.at[a - 1, pl.ds(i * half, half)], xin.at[a - 1, pl.ds(i * half, half)],
                   xs_sem.at[a - 1, i], xr_sem.at[a - 1, i], at(lax.rem(x - a + SIDE, SIDE), y))
            for i in range(2)
        ]
        for a in (1, 2)
    }

    def grads_step(i, carry):
        j = SLOTS - 1 - i
        a, ky, d, valid = slot(j)

        @pl.when(j == 1)
        def _():
            x_hand_over(2)

        @pl.when(valid)
        def _():
            plow, slow = [], []
            for g in range(8):
                sl = slice(g * R, (g + 1) * R)
                factor = jnp.exp2(mrun[j, g:g + 1, :] - norm[g:g + 1, :])
                p = prob[j, :, sl] * factor
                plow.append(p.astype(jnp.bfloat16))
                slow.append((p * (dprob[j, :, sl] - norm[8 + g:9 + g, :])).astype(jnp.bfloat16))
            dk = jnp.dot(jnp.concatenate(slow, axis=1), qc[...], preferred_element_type=jnp.float32)
            dv = jnp.dot(jnp.concatenate(plow, axis=1), oc[...], preferred_element_type=jnp.float32)

            @pl.when(ky == y)
            def _():
                accf[a, :, 0:HD] = dk
                accf[a, :, HD:2 * HD] = dv

            @pl.when(ky != y)
            def _():
                part[j, :, 0:HD] = dk.astype(jnp.bfloat16)
                part[j, :, HD:2 * HD] = dv.astype(jnp.bfloat16)
                for copy in part_copy(j):
                    copy.start()

            for g in range(8):
                gscore[j, :, g * R:(g + 1) * R] = slow[g]

        return carry

    lax.fori_loop(0, SLOTS, grads_step, 0)

    def query_step(j, carry):
        a, ky, d, valid = slot(j)

        @pl.when(valid)
        def _():
            keys = kv[j, :, 0:HD]
            for r in range(4):
                dqt[r] += lax.dot_general(
                    keys, gscore[j, :, r * 2 * R:(r + 1) * 2 * R],
                    (((0,), (0,)), ((), ())), preferred_element_type=jnp.float32,
                )

        return carry

    lax.fori_loop(0, SLOTS, query_step, 0)

    dq_swaps = [
        remote(dqt.at[2 * i + 1], dq_in.at[i], ds_sem.at[i], dr_sem.at[i], mate) for i in range(2)
    ]
    for copy in dq_swaps:
        copy.start()

    x_hand_over(1)
    for copy in dq_swaps:
        copy.wait()
    zq_out[...] = (dqt[2] + dq_in[1]).astype(jnp.bfloat16)
    zq_swap = remote(zq_out, zq_in, ds_sem.at[2], dr_sem.at[2], zmate)
    zq_swap.start()

    for i in range(2):
        for e in range(1, SIDE):
            gather_row(0, e, i, holds & (y + e < SIDE))

    for a in (1, 2):
        @pl.when(holds & (x + a < SIDE))
        def _():
            for i in range(2):
                rows = xin.at[a - 1, pl.ds(i * half, half)]
                remote(rows, rows, xs_sem.at[0, 0], xr_sem.at[a - 1, i], mate).wait_recv()
            accf[0] += xin[a - 1].astype(jnp.float32)

    @pl.when(far_out)
    def _():
        part_arrived(3, 0, 0)
        part_arrived(3, 0, 1)
        accf[0] += got[3, 0].astype(jnp.float32)

    wide_out = HD // share
    pair = lax.div(member, 2)
    z_sends = []
    for e in range(1, share):
        to = lax.rem(member + e, share)
        z_sends.append(
            remote(zout.at[to], zin.at[pair], zs_sem.at[to], zr_sem.at[pair], (grp - member + to, srv))
        )

    @pl.when(holds)
    def _():
        turned = accf[0].T
        for m in range(share):
            for s in range(2):
                piece = turned[s * HD + m * wide_out:s * HD + (m + 1) * wide_out, :]
                zown[m, s * wide_out:(s + 1) * wide_out, :] = piece
                zout[m, s * wide_out:(s + 1) * wide_out, :] = piece.astype(jnp.bfloat16)
        for copy in z_sends:
            copy.start()
        zsum[...] = zown[member]

    @pl.when(jnp.logical_not(holds))
    def _():
        zsum[...] = jnp.zeros_like(zsum)

    zq_swap.wait()
    mixed = dqt[0] + dq_in[0] + zq_in[...].astype(jnp.float32)
    for h in range(2):
        dq_out[:, h * HD:(h + 1) * HD] = (mixed[:, h * R:(h + 1) * R].T * SCALE).astype(jnp.bfloat16)

    for w in range(share // 2):
        @pl.when(jnp.logical_not(holds & (pair == w)))
        def _():
            remote(zin.at[w], zin.at[w], zs_sem.at[0], zr_sem.at[w], mate).wait_recv()
            zsum[...] += zin[w].astype(jnp.float32)

    dk_out[...] = (zsum[0:wide_out, :] * SCALE).astype(jnp.bfloat16)
    dv_out[...] = zsum[wide_out:2 * wide_out, :].astype(jnp.bfloat16)

    for cond, copies in own_sends + near_sends + next_sends + [(x_here[a], x_copy[a]) for a in (1, 2)]:
        for copy in copies:
            pl.when(cond)(copy.wait_send)

    def parts_sent(j, carry):
        a, ky, d, valid = slot(j)

        @pl.when(valid & (ky != y))
        def _():
            for copy in part_copy(j):
                copy.wait_send()

        return carry

    lax.fori_loop(0, SLOTS, parts_sent, 0)
    for copy in z_sends:
        pl.when(holds)(copy.wait_send)


def write_out(a_ref, b_ref, c_ref, a_out, b_out, c_out, sem):
    copies = [
        pltpu.make_async_copy(src, dst, sem.at[i])
        for i, (src, dst) in enumerate(((a_ref, a_out), (b_ref, b_out), (c_ref, c_out)))
    ]
    for copy in copies:
        copy.start()
    for copy in copies:
        copy.wait()


def on_device(queries, key_rows, value_rows, grad_output, doc_ids):
    R = queries.shape[0]
    share = lax.axis_size("grp") // (key_rows.shape[1] // HD)
    wide = min(128, R)
    docs = doc_ids.reshape(-1, wide)
    bf, f32, i32 = jnp.bfloat16, jnp.float32, jnp.int32
    dma = pltpu.SemaphoreType.DMA
    scratch = [
        pltpu.VMEM(docs.shape, i32),
        pltpu.VMEM((SLOTS, R, 2 * HD), bf),
        pltpu.VMEM((8 * R, HD), bf),
        pltpu.VMEM((8 * R, HD), bf),
        pltpu.VMEM((2 * HD, 8 * R), bf),
        pltpu.VMEM((HD, 8 * R), bf),
        pltpu.VMEM((SLOTS, R, HD), bf),
        pltpu.VMEM((2, R), i32),
        pltpu.VMEM((SLOTS, R, 8 * R), f32),
        pltpu.VMEM((SLOTS, R, 8 * R), f32),
        pltpu.VMEM((SLOTS, 8, R), f32),
        pltpu.VMEM((SLOTS, R, 8 * R), bf),
        pltpu.VMEM((24, R), f32),
        pltpu.VMEM((3, 24, R), f32),
        pltpu.VMEM((16, R), f32),
        pltpu.VMEM((4, HD, 2 * R), f32),
        pltpu.VMEM((2, HD, 2 * R), f32),
        pltpu.VMEM((HD, 2 * R), bf),
        pltpu.VMEM((HD, 2 * R), bf),
        pltpu.VMEM((SLOTS, R, 2 * HD), bf),
        pltpu.VMEM((4, SIDE, R, 2 * HD), bf),
        pltpu.VMEM((3, R, 2 * HD), f32),
        pltpu.VMEM((2, R, 2 * HD), bf),
        pltpu.VMEM((2, R, 2 * HD), bf),
        pltpu.VMEM((share, 2 * HD // share, R), f32),
        pltpu.VMEM((share, 2 * HD // share, R), bf),
        pltpu.VMEM((share // 2, 2 * HD // share, R), bf),
        pltpu.VMEM((2 * HD // share, R), f32),
        dma((7,)), dma((6,)), dma((6,)), dma((12, 2)), dma((SLOTS, 2)), dma((3,)), dma((3,)),
        dma((SLOTS, 2)), dma((4, SIDE, 2)), dma((2, 2)), dma((2, 2)), dma((share,)), dma((share // 2,)),
        dma((3,)), dma((3,)), pltpu.SemaphoreType.REGULAR,
    ]
    vmem = pl.BlockSpec(memory_space=pltpu.VMEM)
    hbm = pl.BlockSpec(memory_space=pltpu.HBM)
    dq, dk, dv = pl.pallas_call(
        functools.partial(kernel, share),
        out_shape=(
            pltpu.VMEM((R, 2 * HD), bf),
            pltpu.VMEM((HD // share, R), bf),
            pltpu.VMEM((HD // share, R), bf),
        ),
        in_specs=[hbm, hbm, hbm, hbm, hbm],
        out_specs=(vmem, vmem, vmem),
        scratch_shapes=scratch,
        compiler_params=pltpu.CompilerParams(
            collective_id=0, has_side_effects=True, vmem_limit_bytes=56 * 1024 * 1024
        ),
    )(*(pltpu.with_memory_space_constraint(t, pltpu.HBM) for t in (queries, key_rows, value_rows, grad_output, docs)))
    dq, dk, dv = pl.pallas_call(
        write_out,
        out_shape=tuple(jax.ShapeDtypeStruct(part.shape, part.dtype) for part in (dq, dk, dv)),
        in_specs=[vmem, vmem, vmem],
        out_specs=(hbm, hbm, hbm),
        scratch_shapes=[dma((3,))],
    )(*(pltpu.with_memory_space_constraint(t, pltpu.VMEM) for t in (dq, dk, dv)))
    return dq, dk.T, dv.T


def solution(mesh):
    in_specs = (P("srv", "grp"), P("srv", None), P("srv", None), P("srv", "grp"), P())
    out_specs = (P("srv", "grp"), P("srv", "grp"), P("srv", "grp"))
    return jax.shard_map(
        on_device, mesh=mesh, in_specs=in_specs, out_specs=out_specs, check_vma=False
    )
```

```python
import functools
import math

import jax
import jax.numpy as jnp
from jax import lax
from jax.experimental import pallas as pl
from jax.experimental.pallas import tpu as pltpu
from jax.sharding import PartitionSpec as P

HD = 128
SIDE = 4
SLOTS = 7
HIDDEN = -1e30
MESH = pl.DeviceIdType.MESH
SCALE = HD ** -0.5
SCALE2 = SCALE * math.log2(math.e)


def kernel(
    share, q_ref, k_ref, v_ref, o_ref, doc_hbm,
    dq_out, dk_out, dv_out,
    doc_ref, kv, qc, oc, qt, ot, marks, high, prob, dprob, mrun, gscore, stat, stat_in, norm,
    dqt, dq_in, zq_out, zq_in, part, got, accf, xout, xin, zown, zout, zin, zsum,
    loc_sem, qs_sem, qr_sem, ks_sem, kr_sem, ss_sem, sr_sem, ps_sem, pr_sem,
    xs_sem, xr_sem, zs_sem, zr_sem, ds_sem, dr_sem, in_sem,
):
    R = q_ref.shape[0]
    grp = lax.axis_index("grp")
    srv = lax.axis_index("srv")
    core = lax.rem(srv, 2)
    chip = lax.div(srv, 2)
    y = lax.rem(chip, SIDE)
    x = lax.div(chip, SIDE)
    member = lax.rem(grp, share)
    kv_head = lax.div(grp, share)
    plane = lax.rem(grp, 2)
    mate = (grp, srv + 1 - 2 * core)
    zmate = (grp + 1 - 2 * plane, srv)
    corner = (grp + 1 - 2 * plane, srv + 1 - 2 * core)
    side = lax.rem(x + y, 2)
    holds = side == plane
    column = lax.div(y, 2)

    def at(cx, cy):
        return (grp, (cx * SIDE + cy) * 2 + core)

    def remote(src, dst, ssem, rsem, device):
        return pltpu.make_async_remote_copy(
            src_ref=src, dst_ref=dst, send_sem=ssem, recv_sem=rsem,
            device_id=device, device_id_type=MESH,
        )

    col = pl.ds(pl.multiple_of(kv_head * HD, HD), HD)
    local_kv = [
        pltpu.make_async_copy(k_ref.at[:, col], kv.at[column, :, pl.ds(0, HD)], loc_sem.at[0]),
        pltpu.make_async_copy(v_ref.at[:, col], kv.at[column, :, pl.ds(HD, HD)], loc_sem.at[1]),
    ]
    local_q = []
    for h in range(2):
        rows = pl.ds(h * R, R)
        cols = pl.ds(h * HD, HD)
        local_q.append(pltpu.make_async_copy(q_ref.at[:, cols], qc.at[rows], loc_sem.at[2 + 2 * h]))
        local_q.append(pltpu.make_async_copy(o_ref.at[:, cols], oc.at[rows], loc_sem.at[3 + 2 * h]))
    local_doc = pltpu.make_async_copy(doc_hbm, doc_ref, loc_sem.at[6])
    local_doc.start()
    for copy in local_kv:
        pl.when(holds)(copy.start)
    for copy in local_q:
        copy.start()

    barrier = pltpu.get_barrier_semaphore()

    def greet(device):
        pl.semaphore_signal(barrier, inc=1, device_id=device, device_id_type=MESH)

    far_out = (chip == 3) & (core == 1) & (plane == 1)
    far_in = (chip == 12) & (core == 1) & (plane == 1)
    everyone = [mate, corner]
    for e in range(1, SIDE):
        everyone += [at(x, lax.rem(y + e, SIDE)), at(lax.rem(x + e, SIDE), y)]
    for e in range(1, share):
        everyone.append((grp - member + lax.rem(member + e, share), srv))

    leader = (member == 0) & (srv == 0)
    beside = ((member == 0) & (srv == 1)) | ((member == 1) & (srv == 0))
    around = (
        ((member == 0) & (core == 0) & (chip > 0) & ((x == 0) | (y == 0)))
        | ((member == 1) & (srv == 1)) | ((member >= 2) & (srv == 0))
    )

    @pl.when(jnp.logical_not(leader))
    def _():
        for device in everyone:
            greet(device)

    @pl.when(far_out)
    def _():
        greet(at(3, 0))

    @pl.when(far_in)
    def _():
        greet(at(0, 3))

    local_doc.wait()
    wide = doc_ref.shape[1]
    per = R // wide
    number = lax.broadcasted_iota(jnp.int32, (32, wide), 0)
    lane = lax.broadcasted_iota(jnp.int32, (1, wide), 1)
    qt[HD + 32:2 * HD, :] = jnp.zeros((HD - 32, 8 * R), jnp.bfloat16)
    for b in range(2):
        block = chip * 2 + (core if b == 0 else 1 - core)
        for t in range(per):
            row = block * per + t
            own = doc_ref[pl.ds(row, 1), :]
            fence = jnp.where(own == number, 0.0, HIDDEN).astype(jnp.bfloat16)
            high[b:b + 1, t * wide:(t + 1) * wide] = lane + row * wide
            for g in (2 * b, 2 * b + 1, 2 * b + 4, 2 * b + 5):
                qt[HD:HD + 32, g * R + t * wide:g * R + (t + 1) * wide] = fence

    stat[0:8, :] = jnp.full((8, R), HIDDEN, jnp.float32)
    stat[8:24, :] = jnp.zeros((16, R), jnp.float32)
    dqt[...] = jnp.zeros_like(dqt)

    far = jnp.where(far_out | far_in, 1, 0)
    pl.semaphore_wait(barrier, 2 + 2 * (SIDE - 1) + share - 1 + far - jnp.where(beside | around, 1, 0))

    @pl.when(leader)
    def _():
        for device in everyone:
            pl.semaphore_signal(in_sem, inc=1, device_id=device, device_id_type=MESH)

    def swap(n, src, dst, device):
        return [
            remote(ref.at[pl.ds(src * 2 * R, 2 * R)], ref.at[pl.ds(dst * 2 * R, 2 * R)],
                   qs_sem.at[2 * n + i], qr_sem.at[2 * n + i], device)
            for i, ref in enumerate((qc, oc))
        ]

    to_core, to_plane, to_corner = swap(0, 0, 1, mate), swap(1, 0, 2, zmate), swap(2, 2, 3, mate)

    def kv_send(n, src, dst, device):
        return [
            remote(kv.at[src, pl.ds(i * half, half)], kv.at[dst, pl.ds(i * half, half)],
                   ks_sem.at[n, i], kr_sem.at[dst, i], device)
            for i in range(2)
        ]

    half = R // 2
    own_sends, near_sends, next_sends = [], [], []
    for e in range(1, 3):
        own_sends.append(
            (holds & (x + e < SIDE), kv_send(e - 1, column, 2 * e + column, at(lax.rem(x + e, SIDE), y)))
        )
    own_sends.append((far_out, kv_send(2, column, 6, at(3, 0))))
    for e in range(1, SIDE):
        there = at(x, lax.rem(y + e, SIDE))
        wraps = y + e >= SIDE
        own_sends.append((holds & jnp.logical_not(wraps), kv_send(2 + e, column, column, there)))
        near_sends.append(
            (jnp.logical_not(holds) & (x >= 1), kv_send(5 + e, 2 + column, 2 + column, there))
        )
        reaches = wraps | (core == 1) if e == 1 else wraps
        next_sends.append((holds & (x >= 2) & reaches, kv_send(8 + e, 4 + column, 4 + column, there)))

    def start_all(sends, i):
        for cond, copies in sends:
            pl.when(cond)(copies[i].start)

    for copy in local_kv:
        pl.when(holds)(copy.wait)
    for i in range(2):
        start_all(own_sends, i)
    for copy in local_q:
        copy.wait()

    @pl.when(beside)
    def _():
        pl.semaphore_wait(in_sem, 1)

    for copy in to_plane + to_core:
        copy.start()
    for copy in to_core:
        copy.wait()
    for b in range(2):
        qt[0:HD, b * 2 * R:(b + 1) * 2 * R] = qc[b * 2 * R:(b + 1) * 2 * R, :].T
        ot[:, b * 2 * R:(b + 1) * 2 * R] = oc[b * 2 * R:(b + 1) * 2 * R, :].T

    def kv_half(j, i):
        rows = kv.at[j, pl.ds(i * half, half)]
        remote(rows, rows, ks_sem.at[0, 0], kr_sem.at[j, i], mate).wait_recv()

    def kv_arrived(j):
        for i in range(2):
            kv_half(j, i)

    def slot(j):
        a = lax.div(j, 2)
        ky = jnp.where(a == 3, SIDE - 1, lax.rem(plane + x + a, 2) + 2 * lax.rem(j, 2))
        d = 4 * a + y - ky
        valid = (x >= a) & (d >= 0) & (d <= 8 + core) & ((a < 3) | (plane == 1))
        return a, ky, d, valid

    row_in_block = lax.broadcasted_iota(jnp.int32, (R, R), 0)

    def mark_documents(j, d):
        for t in range(per):
            own = doc_ref[pl.ds(((chip - d) * 2 + core) * per + t, 1), :]
            hot = jnp.where(own == number, 1.0, 0.0)
            hot = jnp.concatenate([hot, jnp.zeros((HD - 32, wide), jnp.float32)], axis=0)
            marks[j, t * wide:(t + 1) * wide, :] = hot.T.astype(jnp.bfloat16)

    def stats_block(z, j, d):
        @pl.when(d == 0)
        def _():
            stats_groups(z, j, True)

        @pl.when(d != 0)
        def _():
            stats_groups(z, j, False)

    def stats_groups(z, j, diagonal):
        key_pos = row_in_block + (chip * 2 + core) * R
        keys = jnp.concatenate([kv[j, :, 0:HD], marks[j]], axis=1)
        values = kv[j, :, HD:2 * HD]
        for g in range(4 * z, 4 * z + 4):
            b = (g // 2) % 2
            sl = slice(g * R, (g + 1) * R)
            s = jnp.dot(keys, qt[:, sl], preferred_element_type=jnp.float32) * SCALE2
            if diagonal:
                s = jnp.where(key_pos <= high[b:b + 1, :], s, HIDDEN)
            m_old = stat[g:g + 1, :]
            m_new = jnp.maximum(m_old, jnp.max(s, axis=0, keepdims=True))
            alpha = jnp.exp2(m_old - m_new)
            p = jnp.exp2(s - m_new)
            dp = jnp.dot(values, ot[:, sl], preferred_element_type=jnp.float32)
            stat[g:g + 1, :] = m_new
            stat[8 + g:9 + g, :] = stat[8 + g:9 + g, :] * alpha + jnp.sum(p, axis=0, keepdims=True)
            stat[16 + g:17 + g, :] = stat[16 + g:17 + g, :] * alpha + jnp.sum(p * dp, axis=0, keepdims=True)
            mrun[j, g:g + 1, :] = m_new
            prob[j, :, sl] = p
            dprob[j, :, sl] = dp

    def stats_step(j, carry):
        @pl.when((j == 1) & (x >= 1) & jnp.logical_not(holds))
        def _():
            for i in range(2):
                kv_half(2 + column, i)
                start_all(near_sends, i)

        @pl.when((j == 2) & (x >= 2) & holds)
        def _():
            for i in range(2):
                kv_half(4 + column, i)
                start_all(next_sends, i)

        @pl.when(j == 4)
        def _():
            for came, goes in zip(to_plane, to_corner):
                came.wait()
                goes.start()

        a, ky, d, valid = slot(j)

        @pl.when(valid)
        def _():
            @pl.when(ky != y)
            def _():
                kv_arrived(j)

            mark_documents(j, d)
            stats_block(0, j, d)

        return carry

    lax.fori_loop(0, SLOTS, stats_step, 0)

    for copy in to_corner:
        copy.wait()
    for b in range(2, 4):
        qt[0:HD, b * 2 * R:(b + 1) * 2 * R] = qc[b * 2 * R:(b + 1) * 2 * R, :].T
        ot[:, b * 2 * R:(b + 1) * 2 * R] = oc[b * 2 * R:(b + 1) * 2 * R, :].T

    def stats_other(j, carry):
        a, ky, d, valid = slot(j)

        @pl.when(valid)
        def _():
            stats_block(1, j, d)

        return carry

    lax.fori_loop(0, SLOTS, stats_other, 0)

    peers = (mate, zmate, corner)
    swaps = [remote(stat, stat_in.at[i], ss_sem.at[i], sr_sem.at[i], peers[i]) for i in range(3)]

    @pl.when(around)
    def _():
        pl.semaphore_wait(in_sem, 1)

    for copy in swaps:
        copy.start()
    for copy in swaps:
        copy.wait()
    for r in range(4):
        def rows_of(kind, r=r):
            mine = [stat[8 * kind + 2 * r:8 * kind + 2 * r + 2, :]]
            for i in range(3):
                there = 8 * kind + 2 * (r ^ (i + 1))
                mine.append(stat_in[i, there:there + 2, :])
            return mine

        tops = rows_of(0)
        top = jnp.maximum(jnp.maximum(tops[0], tops[1]), jnp.maximum(tops[2], tops[3]))
        factors = [jnp.exp2(t - top) for t in tops]
        total = sum(f * t for f, t in zip(factors, rows_of(1)))
        weighted = sum(f * t for f, t in zip(factors, rows_of(2)))
        norm[2 * r:2 * r + 2, :] = top + jnp.log2(total)
        norm[8 + 2 * r:8 + 2 * r + 2, :] = weighted / total

    def part_copy(j):
        a, ky, d, valid = slot(j)
        tx = x - 3 * lax.div(a, 3)
        return [
            remote(part.at[j, pl.ds(i * half, half)], got.at[a, y, pl.ds(i * half, half)],
                   ps_sem.at[j, i], pr_sem.at[a, y, i], at(tx, ky))
            for i in range(2)
        ]

    def part_arrived(a, sy, i):
        rows = got.at[a, sy, pl.ds(i * half, half)]
        remote(rows, rows, ps_sem.at[0, 0], pr_sem.at[a, sy, i], mate).wait_recv()

    def gather_row(a, e, i, cond):
        sy = lax.rem(y + e, SIDE)
        rows = slice(i * half, (i + 1) * half)

        @pl.when(cond)
        def _():
            part_arrived(a, sy, i)
            accf[a, rows, :] += got[a, sy, rows, :].astype(jnp.float32)

    def x_hand_over(a):
        for i in range(2):
            rows = slice(i * half, (i + 1) * half)
            for e in range(1, SIDE):
                wraps = y + e >= SIDE
                reaches = True if a == 1 else (wraps | (core == 1) if e == 1 else wraps)
                gather_row(a, e, i, x_here[a] & reaches)

            @pl.when(x_here[a])
            def _(i=i, rows=rows):
                xout[a - 1, rows, :] = accf[a, rows, :].astype(jnp.bfloat16)
                x_copy[a][i].start()

    x_here = {1: (x >= 1) & jnp.logical_not(holds), 2: (x >= 2) & holds}
    x_copy = {
        a: [
            remote(xout.at[a - 1, pl.ds(i * half, half)], xin.at[a - 1, pl.ds(i * half, half)],
                   xs_sem.at[a - 1, i], xr_sem.at[a - 1, i], at(lax.rem(x - a + SIDE, SIDE), y))
            for i in range(2)
        ]
        for a in (1, 2)
    }

    def grads_step(i, carry):
        j = SLOTS - 1 - i
        a, ky, d, valid = slot(j)

        @pl.when(j == 1)
        def _():
            x_hand_over(2)

        @pl.when(valid)
        def _():
            plow, slow = [], []
            for g in range(8):
                sl = slice(g * R, (g + 1) * R)
                factor = jnp.exp2(mrun[j, g:g + 1, :] - norm[g:g + 1, :])
                p = prob[j, :, sl] * factor
                plow.append(p.astype(jnp.bfloat16))
                slow.append((p * (dprob[j, :, sl] - norm[8 + g:9 + g, :])).astype(jnp.bfloat16))
            dk = jnp.dot(jnp.concatenate(slow, axis=1), qc[...], preferred_element_type=jnp.float32)
            dv = jnp.dot(jnp.concatenate(plow, axis=1), oc[...], preferred_element_type=jnp.float32)

            @pl.when(ky == y)
            def _():
                accf[a, :, 0:HD] = dk
                accf[a, :, HD:2 * HD] = dv

            @pl.when(ky != y)
            def _():
                part[j, :, 0:HD] = dk.astype(jnp.bfloat16)
                part[j, :, HD:2 * HD] = dv.astype(jnp.bfloat16)
                for copy in part_copy(j):
                    copy.start()

            for g in range(8):
                gscore[j, :, g * R:(g + 1) * R] = slow[g]

        return carry

    lax.fori_loop(0, SLOTS, grads_step, 0)

    def query_step(j, carry):
        a, ky, d, valid = slot(j)

        @pl.when(valid)
        def _():
            keys = kv[j, :, 0:HD]
            for r in range(4):
                dqt[r] += lax.dot_general(
                    keys, gscore[j, :, r * 2 * R:(r + 1) * 2 * R],
                    (((0,), (0,)), ((), ())), preferred_element_type=jnp.float32,
                )

        return carry

    lax.fori_loop(0, SLOTS, query_step, 0)

    dq_swaps = [
        remote(dqt.at[2 * i + 1], dq_in.at[i], ds_sem.at[i], dr_sem.at[i], mate) for i in range(2)
    ]
    for copy in dq_swaps:
        copy.start()

    x_hand_over(1)
    for copy in dq_swaps:
        copy.wait()
    zq_out[...] = (dqt[2] + dq_in[1]).astype(jnp.bfloat16)
    zq_swap = remote(zq_out, zq_in, ds_sem.at[2], dr_sem.at[2], zmate)
    zq_swap.start()

    wide_out = HD // share
    pair = lax.div(member, 2)
    z_sends = []
    for i in range(2):
        rows = slice(i * half, (i + 1) * half)
        for e in range(1, SIDE):
            gather_row(0, e, i, holds & (y + e < SIDE))
        for a in (1, 2):
            @pl.when(holds & (x + a < SIDE))
            def _(a=a, i=i, rows=rows):
                came = xin.at[a - 1, pl.ds(i * half, half)]
                remote(came, came, xs_sem.at[0, 0], xr_sem.at[a - 1, i], mate).wait_recv()
                accf[0, rows, :] += xin[a - 1, rows, :].astype(jnp.float32)

        @pl.when(far_out)
        def _(i=i, rows=rows):
            part_arrived(3, 0, i)
            accf[0, rows, :] += got[3, 0, rows, :].astype(jnp.float32)

        goes = []
        for e in range(1, share):
            to = lax.rem(member + e, share)
            goes.append(
                remote(zout.at[i, to], zin.at[i, pair], zs_sem.at[to, i], zr_sem.at[pair, i], (grp - member + to, srv))
            )
        z_sends += goes

        @pl.when(holds)
        def _(i=i, rows=rows, goes=goes):
            turned = accf[0, rows, :].T
            for m in range(share):
                for s in range(2):
                    piece = turned[s * HD + m * wide_out:s * HD + (m + 1) * wide_out, :]
                    zown[m, s * wide_out:(s + 1) * wide_out, rows] = piece
                    zout[i, m, s * wide_out:(s + 1) * wide_out, :] = piece.astype(jnp.bfloat16)
            for copy in goes:
                copy.start()

    @pl.when(holds)
    def _():
        zsum[...] = zown[member]

    @pl.when(jnp.logical_not(holds))
    def _():
        zsum[...] = jnp.zeros_like(zsum)

    zq_swap.wait()
    mixed = dqt[0] + dq_in[0] + zq_in[...].astype(jnp.float32)
    for h in range(2):
        dq_out[:, h * HD:(h + 1) * HD] = (mixed[:, h * R:(h + 1) * R].T * SCALE).astype(jnp.bfloat16)

    for w in range(share // 2):
        @pl.when(jnp.logical_not(holds & (pair == w)))
        def _():
            for i in range(2):
                remote(zin.at[i, w], zin.at[i, w], zs_sem.at[0, 0], zr_sem.at[w, i], mate).wait_recv()
                zsum[:, i * half:(i + 1) * half] += zin[i, w].astype(jnp.float32)

    dk_out[...] = (zsum[0:wide_out, :] * SCALE).astype(jnp.bfloat16)
    dv_out[...] = zsum[wide_out:2 * wide_out, :].astype(jnp.bfloat16)

    for cond, copies in own_sends + near_sends + next_sends + [(x_here[a], x_copy[a]) for a in (1, 2)]:
        for copy in copies:
            pl.when(cond)(copy.wait_send)

    def parts_sent(j, carry):
        a, ky, d, valid = slot(j)

        @pl.when(valid & (ky != y))
        def _():
            for copy in part_copy(j):
                copy.wait_send()

        return carry

    lax.fori_loop(0, SLOTS, parts_sent, 0)
    for copy in z_sends:
        pl.when(holds)(copy.wait_send)


def write_out(a_ref, b_ref, c_ref, a_out, b_out, c_out, sem):
    copies = [
        pltpu.make_async_copy(src, dst, sem.at[i])
        for i, (src, dst) in enumerate(((a_ref, a_out), (b_ref, b_out), (c_ref, c_out)))
    ]
    for copy in copies:
        copy.start()
    for copy in copies:
        copy.wait()


def on_device(queries, key_rows, value_rows, grad_output, doc_ids):
    R = queries.shape[0]
    share = lax.axis_size("grp") // (key_rows.shape[1] // HD)
    wide = min(128, R)
    docs = doc_ids.reshape(-1, wide)
    bf, f32, i32 = jnp.bfloat16, jnp.float32, jnp.int32
    dma = pltpu.SemaphoreType.DMA
    scratch = [
        pltpu.VMEM(docs.shape, i32),
        pltpu.VMEM((SLOTS, R, 2 * HD), bf),
        pltpu.VMEM((8 * R, HD), bf),
        pltpu.VMEM((8 * R, HD), bf),
        pltpu.VMEM((2 * HD, 8 * R), bf),
        pltpu.VMEM((HD, 8 * R), bf),
        pltpu.VMEM((SLOTS, R, HD), bf),
        pltpu.VMEM((2, R), i32),
        pltpu.VMEM((SLOTS, R, 8 * R), f32),
        pltpu.VMEM((SLOTS, R, 8 * R), f32),
        pltpu.VMEM((SLOTS, 8, R), f32),
        pltpu.VMEM((SLOTS, R, 8 * R), bf),
        pltpu.VMEM((24, R), f32),
        pltpu.VMEM((3, 24, R), f32),
        pltpu.VMEM((16, R), f32),
        pltpu.VMEM((4, HD, 2 * R), f32),
        pltpu.VMEM((2, HD, 2 * R), f32),
        pltpu.VMEM((HD, 2 * R), bf),
        pltpu.VMEM((HD, 2 * R), bf),
        pltpu.VMEM((SLOTS, R, 2 * HD), bf),
        pltpu.VMEM((4, SIDE, R, 2 * HD), bf),
        pltpu.VMEM((3, R, 2 * HD), f32),
        pltpu.VMEM((2, R, 2 * HD), bf),
        pltpu.VMEM((2, R, 2 * HD), bf),
        pltpu.VMEM((share, 2 * HD // share, R), f32),
        pltpu.VMEM((2, share, 2 * HD // share, R // 2), bf),
        pltpu.VMEM((2, share // 2, 2 * HD // share, R // 2), bf),
        pltpu.VMEM((2 * HD // share, R), f32),
        dma((7,)), dma((6,)), dma((6,)), dma((12, 2)), dma((SLOTS, 2)), dma((3,)), dma((3,)),
        dma((SLOTS, 2)), dma((4, SIDE, 2)), dma((2, 2)), dma((2, 2)), dma((share, 2)), dma((share // 2, 2)),
        dma((3,)), dma((3,)), pltpu.SemaphoreType.REGULAR,
    ]
    vmem = pl.BlockSpec(memory_space=pltpu.VMEM)
    hbm = pl.BlockSpec(memory_space=pltpu.HBM)
    dq, dk, dv = pl.pallas_call(
        functools.partial(kernel, share),
        out_shape=(
            pltpu.VMEM((R, 2 * HD), bf),
            pltpu.VMEM((HD // share, R), bf),
            pltpu.VMEM((HD // share, R), bf),
        ),
        in_specs=[hbm, hbm, hbm, hbm, hbm],
        out_specs=(vmem, vmem, vmem),
        scratch_shapes=scratch,
        compiler_params=pltpu.CompilerParams(
            collective_id=0, has_side_effects=True, vmem_limit_bytes=56 * 1024 * 1024
        ),
    )(*(pltpu.with_memory_space_constraint(t, pltpu.HBM) for t in (queries, key_rows, value_rows, grad_output, docs)))
    dq, dk, dv = pl.pallas_call(
        write_out,
        out_shape=tuple(jax.ShapeDtypeStruct(part.shape, part.dtype) for part in (dq, dk, dv)),
        in_specs=[vmem, vmem, vmem],
        out_specs=(hbm, hbm, hbm),
        scratch_shapes=[dma((3,))],
    )(*(pltpu.with_memory_space_constraint(t, pltpu.VMEM) for t in (dq, dk, dv)))
    return dq, dk.T, dv.T


def solution(mesh):
    in_specs = (P("srv", "grp"), P("srv", None), P("srv", None), P("srv", "grp"), P())
    out_specs = (P("srv", "grp"), P("srv", "grp"), P("srv", "grp"))
    return jax.shard_map(
        on_device, mesh=mesh, in_specs=in_specs, out_specs=out_specs, check_vma=False
    )
```
